512 devices in a mesh: tm: 64 (over y, z), head: 8 (over x, core).
Axes of the slice: x: 4, y: 4, z: 16, core: 2. Of those that a mesh axis runs over, the one named last changes fastest.
Arguments:
- queries: bfloat16 [16384, 3072], P('tm', 'head'), may hold values from -170 to 170
- key_rows: bfloat16 [16384, 3072], P('tm', 'head'), may hold values from -6 to 6
- value_rows: bfloat16 [16384, 3072], P('tm', 'head'), may hold values from -102 to 102
- grad_normed: bfloat16 [16384, 3072], P('tm', 'head'), may hold values from -5.5 to 5.5
- norm_gain: float32 [3072], P('head'), may hold values from 0.25 to 1.75
- utter_ids: int32 [128], P('tm'), may hold values from 0 to 20, never falling along the last dimension, each value on 1 to 8 neighbouring positions
Outputs:
- normed: bfloat16 [16384, 3072], P('tm', 'head')
- grad_queries: bfloat16 [16384, 3072], P('tm', 'head')
- grad_keys: bfloat16 [16384, 3072], P('tm', 'head')
- grad_values: bfloat16 [16384, 3072], P('tm', 'head')
- grad_gain: float32 [3072], P('head')
The draws below stay inside these ranges and needn't reach their ends.
Inputs may be any that keep to these rules, and one draw needn't show every extreme that they name: `utter_ids`: ids never fall; each utterance covers 1 to 8 consecutive blocks of 128 frames, and one covers exactly 8.
All inputs are finite; a program needn't handle non-finite values.
Results may differ from the reference program's by a relative error of at most 0.024.
Values may be sent and summed in bfloat16 or wider, within the bound.
A program may use at most 64 MiB of HBM per device.

```python
import math
import jax
import jax.numpy as jnp
import numpy as np
from jax import lax

HSZ = 128
GROUP = 256
BLK = 128
MOST_BLK = 8
REACH = 4
TOTAL = 16384
NBLK = 128
HEADS = 24
WIDTH = 3072
N_TM = 64


def paired_rows(key):
    base_key = jax.random.fold_in(key, 7)
    full_shape = (TOTAL, HEADS * HSZ)
    key_part = jnp.clip(jax.random.normal(jax.random.fold_in(base_key, 1), full_shape, jnp.float32), -6.0, 6.0)
    query_part = jnp.clip(jax.random.normal(jax.random.fold_in(base_key, 2), full_shape, jnp.float32), -6.0, 6.0)
    return (key_part, query_part)


def draw_key_rows(key, part):
    key_part, query_part = paired_rows(key)
    return key_part.astype(jnp.bfloat16)


def draw_queries(key, part):
    key_part, query_part = paired_rows(key)
    return query_part.astype(jnp.bfloat16)


def draw_value_rows(key, part):
    full_shape = (TOTAL, HEADS * HSZ)
    column = (jnp.arange(HEADS * HSZ) // HSZ).astype(jnp.float32)
    rising = jnp.exp(column * (math.log(3.0) / max(HEADS - 1, 1)))
    spread = jax.random.uniform(jax.random.fold_in(key, 2), (HEADS * HSZ,), jnp.float32, 0.0, 1.0)
    col_scale = rising * jnp.exp(spread * math.log(3.3))
    raw_rows = jnp.clip(jax.random.normal(jax.random.fold_in(key, 1), full_shape, jnp.float32), -6.0, 6.0)
    return (raw_rows * col_scale[None, :]).astype(jnp.bfloat16)


def draw_grad_normed(key, part):
    full_shape = (TOTAL, HEADS * HSZ)
    frames = jnp.arange(TOTAL).astype(jnp.float32)
    rising = jnp.exp(frames * (math.log(3.0) / max(TOTAL - 1, 1)))[:, None]
    raw_rows = jnp.clip(jax.random.normal(jax.random.fold_in(key, 1), full_shape, jnp.float32), -6.0, 6.0)
    return (0.3 * raw_rows * rising).astype(jnp.bfloat16)


def split_up(count, total, bound, skew):
    weights = [(1 << 20) // math.isqrt(grade ** skew) + 1 for grade in range(2, count + 1)]
    surplus, counts = total - bound - (count - 1), [1] * (count - 1)
    while surplus > 0:
        movable = [i for i in range(count - 1) if counts[i] < bound]
        whole, left = sum([weights[i] for i in movable]), surplus
        for i in movable:
            more = min(bound - counts[i], max(1, left * weights[i] // whole), surplus)
            counts[i] = counts[i] + more
            surplus = surplus - more
    return np.array([bound] + counts)


def ragged(rng, number_of, total, reach, slope):
    if number_of == 2:
        one = jax.random.randint(rng, (), max(1, total - reach), min(reach, total - 1) + 1)
        return jnp.stack([one, total - one])
    sizes = jnp.asarray(split_up(number_of, total, reach, slope), jnp.int32)
    twos = (number_of - 1) // 2
    donor, sink = sizes[1:1 + 2 * twos:2], sizes[2:2 + 2 * twos:2]
    slack = jnp.minimum(donor - 1, reach - sink)
    passed = jax.random.randint(jax.random.fold_in(rng, 1), (twos,), 0, 1 << 20) % (slack + 1)
    sizes = sizes.at[1:1 + 2 * twos:2].set(donor - passed).at[2:2 + 2 * twos:2].set(sink + passed)
    return sizes[jax.random.permutation(jax.random.fold_in(rng, 2), number_of)]


def setup_inputs(seed: int = 0) -> dict:
    seeds = jax.random.split(jax.random.key(seed), 7)
    return {
        "queries": draw_queries(jax.random.fold_in(seeds[6], 71), 0),
        "key_rows": draw_key_rows(jax.random.fold_in(seeds[6], 71), 0),
        "value_rows": draw_value_rows(jax.random.fold_in(seeds[6], 71), 0),
        "grad_normed": draw_grad_normed(jax.random.fold_in(seeds[6], 71), 0),
        "norm_gain": jnp.clip(1.0 + 0.15 * jax.random.normal(seeds[4], (WIDTH,), jnp.float32), 0.25, 1.75),
        "utter_ids": jnp.searchsorted(jnp.cumsum(ragged(seeds[5], NBLK // 6, NBLK, MOST_BLK, 2)), jnp.arange(NBLK), side="right").astype(jnp.int32),
    }


def masked_scores(query_part, key_part, query_utt, key_utt, factor):
    scores = jnp.einsum('qhe,khe->hqk', query_part, key_part) * factor
    allowed = query_utt[:, None] == key_utt[None, :]
    return jnp.where(allowed[None], scores, -jnp.inf)

def rounded(operand):
    return lax.optimization_barrier(operand.astype(jnp.bfloat16)).astype(jnp.float32)

def reference(queries, key_rows, value_rows, grad_normed, norm_gain, utter_ids):
    factor = HSZ ** (-0.5)
    layout = (TOTAL, HEADS, HSZ)
    margin = REACH * GROUP
    window = margin + GROUP
    frame_utt = jnp.repeat(utter_ids.astype(jnp.int32), BLK)
    query_heads = queries.reshape(layout)
    pad_heads = jnp.zeros((margin, HEADS, HSZ), jnp.bfloat16)
    key_pad = jnp.concatenate([pad_heads, key_rows.reshape(layout)], axis=0)
    value_pad = jnp.concatenate([pad_heads, value_rows.reshape(layout)], axis=0)
    utt_pad = jnp.concatenate([jnp.full((margin,), -1, jnp.int32), frame_utt])
    group_ids = jnp.arange(N_TM, dtype=jnp.int32)

    def gather_group(group_index):
        first_row = (group_index * GROUP).astype(jnp.int32)
        query_part = lax.dynamic_slice_in_dim(query_heads, first_row, GROUP, 0).astype(jnp.float32)
        key_part = lax.dynamic_slice_in_dim(key_pad, first_row, window, 0).astype(jnp.float32)
        value_part = lax.dynamic_slice_in_dim(value_pad, first_row, window, 0).astype(jnp.float32)
        query_utt = lax.dynamic_slice_in_dim(frame_utt, first_row, GROUP, 0)
        key_utt = lax.dynamic_slice_in_dim(utt_pad, first_row, window, 0)
        return (first_row, query_part, key_part, value_part, query_utt, key_utt)

    def forward(group_index):
        first_row, query_part, key_part, value_part, query_utt, key_utt = gather_group(group_index)
        scores = masked_scores(query_part, key_part, query_utt, key_utt, factor)
        top_score = lax.optimization_barrier(jnp.max(scores, axis=2))
        log_total = top_score + jnp.log(lax.optimization_barrier(jnp.sum(jnp.exp(scores - top_score[:, :, None]), axis=2)))
        weights = rounded(jnp.exp(scores - log_total[:, :, None]))
        attended = jnp.einsum('hqk,khe->qhe', weights, value_part).astype(jnp.bfloat16)
        return (attended, log_total)
    attended, log_totals = lax.map(forward, group_ids)
    flat_att = attended.reshape(TOTAL, HEADS * HSZ).astype(jnp.float32)
    gain_f32 = norm_gain.astype(jnp.float32)
    square_mean = lax.optimization_barrier(jnp.mean(flat_att * flat_att, axis=1))
    rms_inv = 1.0 / jnp.sqrt(square_mean + 1e-06)
    normed = (flat_att * rms_inv[:, None] * gain_f32).astype(jnp.bfloat16)
    grad_rows = grad_normed.astype(jnp.float32)
    scaled = grad_rows * gain_f32
    cross_mean = lax.optimization_barrier(jnp.mean(scaled * flat_att, axis=1))
    grad_att = (rms_inv[:, None] * (scaled - flat_att * (rms_inv * rms_inv * cross_mean)[:, None])).astype(jnp.bfloat16)
    grad_gain = lax.optimization_barrier(jnp.sum(grad_rows * flat_att * rms_inv[:, None], axis=0))
    grad_heads = grad_att.reshape(layout)
    att_heads = attended.reshape(layout)

    def backward(accums, group_index):
        first_row, query_part, key_part, value_part, query_utt, key_utt = gather_group(group_index)
        grad_part = lax.dynamic_slice_in_dim(grad_heads, first_row, GROUP, 0).astype(jnp.float32)
        att_part = lax.dynamic_slice_in_dim(att_heads, first_row, GROUP, 0).astype(jnp.float32)
        row_delta = lax.optimization_barrier(jnp.sum(att_part * grad_part, axis=2)).T
        log_total = log_totals[group_index]
        scores = masked_scores(query_part, key_part, query_utt, key_utt, factor)
        weights_f32 = jnp.exp(scores - log_total[:, :, None])
        weights = rounded(weights_f32)
        grad_weights = jnp.einsum('qhe,khe->hqk', grad_part, value_part)
        dscore = rounded(weights_f32 * (grad_weights - row_delta[:, :, None]))
        grad_query = (jnp.einsum('hqk,khe->qhe', dscore, key_part) * factor).astype(jnp.bfloat16)
        key_grad = rounded(jnp.einsum('hqk,qhe->khe', dscore, query_part) * factor)
        value_grad = rounded(jnp.einsum('hqk,qhe->khe', weights, grad_part))
        key_accum = lax.dynamic_update_slice_in_dim(accums[0], lax.dynamic_slice_in_dim(accums[0], first_row, window, 0) + key_grad, first_row, 0)
        value_accum = lax.dynamic_update_slice_in_dim(accums[1], lax.dynamic_slice_in_dim(accums[1], first_row, window, 0) + value_grad, first_row, 0)
        return ((key_accum, value_accum), grad_query)
    zero_pad = jnp.zeros((TOTAL + margin, HEADS, HSZ), jnp.float32)
    accums, grad_groups = lax.scan(backward, (zero_pad, zero_pad), group_ids)
    grad_queries = grad_groups.reshape(TOTAL, HEADS * HSZ)
    grad_keys = accums[0][margin:].reshape(TOTAL, HEADS * HSZ).astype(jnp.bfloat16)
    grad_values = accums[1][margin:].reshape(TOTAL, HEADS * HSZ).astype(jnp.bfloat16)
    return (normed, grad_queries, grad_keys, grad_values, grad_gain)
```

```python
import functools

import jax
import jax.numpy as jnp
from jax import lax
from jax.experimental import pallas as pl
from jax.experimental.pallas import tpu as pltpu
from jax.sharding import PartitionSpec as P

HSZ = 128
BLK = 128
REACH = 4
NEG = -1e30
MESH = pl.DeviceIdType.MESH
F32 = jnp.float32
BF16 = jnp.bfloat16


def nt(a, b):
    return lax.dot_general(a, b, (((1,), (1,)), ((), ())), preferred_element_type=F32)


def tn(a, b):
    return lax.dot_general(a, b, (((0,), (0,)), ((), ())), preferred_element_type=F32)


def nn(a, b):
    return lax.dot_general(a, b, (((1,), (0,)), ((), ())), preferred_element_type=F32)


def radices(count):
    found, stride = [], 1
    while stride < count:
        radix = min(4, count // stride)
        found.append((stride, radix))
        stride *= radix
    return found


def kernel(
    n_tm,
    n_head,
    heads,
    stages,
    q_hbm,
    k_hbm,
    v_hbm,
    g_hbm,
    gain_ref,
    ids_ref,
    normed_ref,
    dq_ref,
    dk_ref,
    dv_ref,
    dgain_ref,
    qb,
    kb,
    vb,
    db,
    q4,
    k4,
    v4,
    d4,
    gb,
    ids_own,
    ids_prev,
    ids_next,
    stats_own,
    stats_next,
    s_ref,
    s4_ref,
    r_ref,
    r4_ref,
    out_acc,
    att_ref,
    sums_own,
    sums_in,
    gain_own,
    gain_in,
    dq_acc,
    dk_acc,
    dv_acc,
    local_sem,
    k_send,
    k_recv,
    q_send,
    q_recv,
    v_send,
    v_recv,
    d_send,
    d_recv,
    ip_send,
    ip_recv,
    in_send,
    in_recv,
    st_send,
    st_recv,
    hd_send,
    hd_recv,
    gn_send,
    gn_recv,
):
    tm = lax.axis_index("tm")
    head = lax.axis_index("head")
    later = (lax.rem(tm + 1, n_tm), head)
    earlier = (lax.rem(tm + n_tm - 1, n_tm), head)
    factor = HSZ ** (-0.5)
    features = HSZ * heads * n_head

    def local(which, src, dst, h):
        return pltpu.make_async_copy(
            src.at[:, h * HSZ : (h + 1) * HSZ], dst.at[h], local_sem.at[which, h]
        )

    loads = []
    for which, (src, dst) in enumerate(
        [(k_hbm, kb.at[0]), (q_hbm, qb.at[0]), (v_hbm, vb.at[0]), (g_hbm, gb)]
    ):
        loads.append([local(which, src, dst, h) for h in range(heads)])
        for one in loads[-1]:
            one.start()

    ids_own[...] = jnp.zeros(ids_own.shape, jnp.int32)
    ids_own[0:1, :] = jnp.full((1, BLK), ids_ref[0], jnp.int32)
    ids_own[1:2, :] = jnp.full((1, BLK), ids_ref[1], jnp.int32)

    def gain_peer(stage, off):
        stride, radix = stages[stage]
        digit = lax.rem(tm // stride, radix)
        return (tm + (lax.rem(digit + off, radix) - digit) * stride, head)

    barrier = pltpu.get_barrier_semaphore()
    greeted = [later, earlier]
    greeted += [(tm, lax.rem(head + off, n_head)) for off in range(1, n_head)]
    for stage, (_, radix) in enumerate(stages):
        greeted += [gain_peer(stage, off) for off in range(1, radix)]
    for peer in greeted:
        pl.semaphore_signal(barrier, inc=1, device_id=peer, device_id_type=MESH)
    pl.semaphore_wait(barrier, len(greeted))

    def remote(src, dst, send, recv, peer):
        return pltpu.make_async_remote_copy(
            src_ref=src,
            dst_ref=dst,
            send_sem=send,
            recv_sem=recv,
            device_id=peer,
            device_id_type=MESH,
        )

    def chain(full, last, send, recv, peer, rows, hop, h):
        if hop < REACH - 1:
            src, dst = full.at[hop, h], full.at[hop + 1, h]
        else:
            src, dst = full.at[hop, h, rows, :], last.at[h]
        return remote(src, dst, send.at[hop, h], recv.at[hop, h], peer)

    low, high = pl.ds(0, BLK), pl.ds(BLK, BLK)
    k_hop = functools.partial(chain, kb, k4, k_send, k_recv, later, high)
    v_hop = functools.partial(chain, vb, v4, v_send, v_recv, later, high)
    q_hop = functools.partial(chain, qb, q4, q_send, q_recv, earlier, low)
    d_hop = functools.partial(chain, db, d4, d_send, d_recv, earlier, low)

    def small_hop(own, got, send, recv, peer, hop):
        src = own if hop == 0 else got.at[hop - 1]
        return remote(src, got.at[hop], send.at[hop], recv.at[hop], peer)

    ip_hop = functools.partial(small_hop, ids_own, ids_prev, ip_send, ip_recv, later)
    in_hop = functools.partial(small_hop, ids_own, ids_next, in_send, in_recv, earlier)
    st_hop = functools.partial(small_hop, stats_own, stats_next, st_send, st_recv, earlier)

    def over_heads(step):
        lax.fori_loop(0, heads, lambda h, c: (step(h), c)[1], 0)

    def bias_row(key_row, query_rows):
        parts = [jnp.where(key_row == row, 0.0, NEG).astype(F32) for row in query_rows]
        return parts[0] if len(parts) == 1 else jnp.concatenate(parts, axis=1)

    ip_hop(0).start()
    in_hop(0).start()
    for h in range(heads):
        loads[0][h].wait()
        k_hop(0, h).start()
        loads[1][h].wait()
        q_hop(0, h).start()

    own_rows = [ids_own[0:1, :], ids_own[1:2, :]]

    def score_block(dst, keys, queries, biases):
        for part in range(2):
            rows = pl.ds(part * BLK, BLK)
            dst[rows, :] = nt(keys[rows, :], queries[...]) * factor + biases[part]

    own_bias = [bias_row(own_rows[p], own_rows) for p in range(2)]
    over_heads(lambda h: score_block(s_ref.at[0, h], kb.at[0, h], qb.at[0, h], own_bias))

    for d in range(1, REACH):
        ip_hop(d - 1).wait_recv()
        ip_hop(d).start()
        in_hop(d - 1).wait_recv()
        in_hop(d).start()
        prev_rows = [ids_prev[d - 1, 0:1, :], ids_prev[d - 1, 1:2, :]]
        next_rows = [ids_next[d - 1, 0:1, :], ids_next[d - 1, 1:2, :]]
        s_bias = [bias_row(prev_rows[p], own_rows) for p in range(2)]
        r_bias = [bias_row(own_rows[p], next_rows) for p in range(2)]

        def arrive(h, d=d, s_bias=s_bias, r_bias=r_bias):
            k_hop(d - 1, h).wait_recv()
            k_hop(d, h).start()
            q_hop(d - 1, h).wait_recv()
            q_hop(d, h).start()
            score_block(s_ref.at[d, h], kb.at[d, h], qb.at[0, h], s_bias)
            score_block(r_ref.at[d - 1, h], kb.at[0, h], qb.at[d, h], r_bias)

        over_heads(arrive)

    for h in range(heads):
        loads[2][h].wait()
        v_hop(0, h).start()
    ip_hop(3).wait_recv()
    in_hop(3).wait_recv()
    s4_bias = bias_row(ids_prev[3, 1:2, :], [own_rows[0]])
    r4_bias = bias_row(own_rows[1], [ids_next[3, 0:1, :]])

    def soften(h):
        k_hop(3, h).wait_recv()
        q_hop(3, h).wait_recv()
        s4 = nt(k4[h], qb[0, h, 0:BLK, :]) * factor + s4_bias
        r4_ref[h] = nt(kb[0, h, BLK : 2 * BLK, :], q4[h]) * factor + r4_bias
        top = jnp.max(s_ref[0, h], axis=0, keepdims=True)
        for d in range(1, REACH):
            top = jnp.maximum(top, jnp.max(s_ref[d, h], axis=0, keepdims=True))
        top4 = jnp.max(s4, axis=0, keepdims=True)
        top_low = jnp.maximum(top[:, 0:BLK], top4)
        top = jnp.concatenate([top_low, top[:, BLK:]], axis=1)
        e4 = jnp.exp(s4 - top_low)
        total4 = jnp.sum(e4, axis=0, keepdims=True)
        total = jnp.concatenate([total4, jnp.zeros((1, BLK), F32)], axis=1)
        for d in range(REACH):
            e = jnp.exp(s_ref[d, h] - top)
            s_ref[d, h] = e
            total = total + jnp.sum(e, axis=0, keepdims=True)
        inverse = 1.0 / total
        for d in range(REACH):
            s_ref[d, h] = s_ref[d, h] * inverse
        s4_ref[h] = e4 * inverse[:, 0:BLK]
        stats_own[pl.ds(h, 1), :] = top + jnp.log(total)
        out_acc[h] = tn(s_ref[0, h].astype(BF16), vb[0, h])

    stats_own[...] = jnp.zeros(stats_own.shape, F32)
    over_heads(soften)

    for d in range(1, REACH):

        def attend(h, d=d):
            v_hop(d - 1, h).wait_recv()
            v_hop(d, h).start()
            out_acc[h] += tn(s_ref[d, h].astype(BF16), vb[d, h])

        over_heads(attend)

    for h in range(heads):
        loads[3][h].wait()
    square = jnp.zeros((2 * BLK, HSZ), F32)
    cross = jnp.zeros((2 * BLK, HSZ), F32)
    for h in range(heads):
        v_hop(3, h).wait_recv()
        out_acc[h, 0:BLK, :] += tn(s4_ref[h].astype(BF16), v4[h])
        att_b = out_acc[h].astype(BF16)
        att_ref[h] = att_b
        att = att_b.astype(F32)
        scaled = gb[h].astype(F32) * gain_ref[:, h * HSZ : (h + 1) * HSZ]
        square = square + att * att
        cross = cross + scaled * att
    sums_own[...] = jnp.zeros(sums_own.shape, F32)
    sums_own[0:1, :] = jnp.sum(square.T, axis=0, keepdims=True)
    sums_own[1:2, :] = jnp.sum(cross.T, axis=0, keepdims=True)

    def head_copy(off):
        return remote(
            sums_own,
            sums_in.at[off - 1],
            hd_send.at[off - 1],
            hd_recv.at[off - 1],
            (tm, lax.rem(head + off, n_head)),
        )

    for off in range(1, n_head):
        head_copy(off).start()
    sums = sums_own[...]
    for off in range(1, n_head):
        head_copy(off).wait_recv()
        sums = sums + sums_in[off - 1]
    rms_row = 1.0 / jnp.sqrt(sums[0:1, :] / features + 1e-06)
    pull_row = rms_row * rms_row * sums[1:2, :] / features
    rms = jnp.broadcast_to(rms_row, (HSZ, 2 * BLK)).T
    pull = jnp.broadcast_to(pull_row, (HSZ, 2 * BLK)).T

    gain_own[...] = jnp.zeros(gain_own.shape, F32)
    for h in range(heads):
        cols = slice(h * HSZ, (h + 1) * HSZ)
        att = att_ref[h].astype(F32)
        grad = gb[h].astype(F32)
        gain = gain_ref[:, cols]
        grad_att = (rms * (grad * gain - att * pull)).astype(BF16)
        db[0, h] = grad_att
        delta = att * grad_att.astype(F32)
        stats_own[heads + h : heads + h + 1, :] = jnp.sum(delta.T, axis=0, keepdims=True)
        d_hop(0, h).start()
        scaled_att = att * rms
        normed_ref[:, cols] = (scaled_att * gain).astype(BF16)
        gain_own[0, h : h + 1, :] = jnp.sum(grad * scaled_att, axis=0, keepdims=True)
    st_hop(0).start()

    def gain_copy(stage, off):
        return remote(
            gain_own.at[stage],
            gain_in.at[stage, off - 1],
            gn_send.at[stage, off - 1],
            gn_recv.at[stage, off - 1],
            gain_peer(stage, off),
        )

    def gain_begin(stage):
        for off in range(1, stages[stage][1]):
            gain_copy(stage, off).start()

    def gain_end(stage):
        total = gain_own[stage]
        for off in range(1, stages[stage][1]):
            gain_copy(stage, off).wait_recv()
            total = total + gain_in[stage, off - 1]
        gain_own[stage + 1] = total

    gain_begin(0)

    def own_block(h):
        weights = s_ref[0, h]
        grad_h = db[0, h]
        delta = stats_own[pl.ds(heads + h, 1), :]
        dscore = (weights * (nt(vb[0, h], grad_h) - delta)).astype(BF16)
        dq_acc[h] = tn(dscore, kb[0, h])
        dk_acc[h] = nn(dscore, qb[0, h])
        dv_acc[h] = nn(weights.astype(BF16), grad_h)

    over_heads(own_block)

    for d in range(1, REACH):
        st_hop(d - 1).wait_recv()
        st_hop(d).start()

        def backward(h, d=d):
            d_hop(d - 1, h).wait_recv()
            d_hop(d, h).start()
            delta = stats_own[pl.ds(heads + h, 1), :]
            dscore = (s_ref[d, h] * (nt(vb[d, h], db[0, h]) - delta)).astype(BF16)
            dq_acc[h] += tn(dscore, kb[d, h])
            log_total = stats_next[d - 1, pl.ds(h, 1), :]
            delta = stats_next[d - 1, pl.ds(heads + h, 1), :]
            weights = jnp.exp(r_ref[d - 1, h] - log_total)
            grad_h = db[d, h]
            dv_acc[h] += nn(weights.astype(BF16), grad_h)
            dscore = (weights * (nt(vb[0, h], grad_h) - delta)).astype(BF16)
            dk_acc[h] += nn(dscore, qb[d, h])

        over_heads(backward)
        if d - 1 < len(stages):
            gain_end(d - 1)
            if d < len(stages):
                gain_begin(d)

    st_hop(3).wait_recv()
    for h in range(heads):
        cols = slice(h * HSZ, (h + 1) * HSZ)
        delta = stats_own[heads + h : heads + h + 1, 0:BLK]
        dscore = (s4_ref[h] * (nt(v4[h], db[0, h, 0:BLK, :]) - delta)).astype(BF16)
        dq_acc[h, 0:BLK, :] += tn(dscore, k4[h])
        dq_ref[:, cols] = (dq_acc[h] * factor).astype(BF16)
    for h in range(heads):
        cols = slice(h * HSZ, (h + 1) * HSZ)
        d_hop(3, h).wait_recv()
        log_total = stats_next[3, h : h + 1, 0:BLK]
        delta = stats_next[3, heads + h : heads + h + 1, 0:BLK]
        weights = jnp.exp(r4_ref[h] - log_total)
        grad_h = d4[h]
        dv_acc[h, BLK : 2 * BLK, :] += nn(weights.astype(BF16), grad_h)
        dscore = (weights * (nt(vb[0, h, BLK : 2 * BLK, :], grad_h) - delta)).astype(BF16)
        dk_acc[h, BLK : 2 * BLK, :] += nn(dscore, q4[h])
        dk_ref[:, cols] = (dk_acc[h] * factor).astype(BF16)
        dv_ref[:, cols] = dv_acc[h].astype(BF16)
        dgain_ref[0:1, cols] = gain_own[len(stages), h : h + 1, :]

    for hop in range(REACH):
        ip_hop(hop).wait_send()
        in_hop(hop).wait_send()
        st_hop(hop).wait_send()
        for h in range(heads):
            k_hop(hop, h).wait_send()
            q_hop(hop, h).wait_send()
            v_hop(hop, h).wait_send()
            d_hop(hop, h).wait_send()
    for off in range(1, n_head):
        head_copy(off).wait_send()
    for stage, (_, radix) in enumerate(stages):
        for off in range(1, radix):
            gain_copy(stage, off).wait_send()


def body(queries, key_rows, value_rows, grad_normed, norm_gain, utter_ids):
    rows, width = queries.shape
    heads = width // HSZ
    n_tm, n_head = lax.axis_size("tm"), lax.axis_size("head")
    stages = radices(n_tm)
    full = pltpu.VMEM((REACH, heads, rows, HSZ), BF16)
    last = pltpu.VMEM((heads, BLK, HSZ), BF16)
    wide = pltpu.VMEM((heads, rows, HSZ), F32)
    dma = pltpu.SemaphoreType.DMA
    hops = [dma((REACH, heads))] * 8 + [dma((REACH,))] * 6
    most = max(radix for _, radix in stages) - 1
    scratch = [full] * 4 + [last] * 4
    scratch += [
        pltpu.VMEM((heads, rows, HSZ), BF16),
        pltpu.VMEM((8, BLK), jnp.int32),
        pltpu.VMEM((REACH, 8, BLK), jnp.int32),
        pltpu.VMEM((REACH, 8, BLK), jnp.int32),
        pltpu.VMEM((8, rows), F32),
        pltpu.VMEM((REACH, 8, rows), F32),
        pltpu.VMEM((REACH, heads, rows, rows), F32),
        pltpu.VMEM((heads, BLK, BLK), F32),
        pltpu.VMEM((REACH - 1, heads, rows, rows), F32),
        pltpu.VMEM((heads, BLK, BLK), F32),
        wide,
        pltpu.VMEM((heads, rows, HSZ), BF16),
        pltpu.VMEM((8, rows), F32),
        pltpu.VMEM((n_head - 1, 8, rows), F32),
        pltpu.VMEM((len(stages) + 1, 8, HSZ), F32),
        pltpu.VMEM((len(stages), most, 8, HSZ), F32),
        wide,
        wide,
        wide,
        dma((4, heads)),
    ]
    scratch += hops
    scratch += [dma((n_head - 1,))] * 2 + [dma((len(stages), most))] * 2
    hbm = pl.BlockSpec(memory_space=pl.ANY)
    vmem = pl.BlockSpec(memory_space=pltpu.VMEM)
    big = jax.ShapeDtypeStruct((rows, width), BF16)
    outs = pl.pallas_call(
        functools.partial(kernel, n_tm, n_head, heads, stages),
        out_shape=[big] * 4 + [jax.ShapeDtypeStruct((1, width), F32)],
        in_specs=[hbm] * 4 + [vmem, pl.BlockSpec(memory_space=pltpu.SMEM)],
        out_specs=[vmem] * 5,
        scratch_shapes=scratch,
        compiler_params=pltpu.CompilerParams(collective_id=0, has_side_effects=True),
        name="attention_step",
    )(queries, key_rows, value_rows, grad_normed, norm_gain.reshape(1, width), utter_ids)
    return (*outs[:4], outs[4].reshape(width))


def solution(mesh):
    in_specs = (
        P("tm", "head"),
        P("tm", "head"),
        P("tm", "head"),
        P("tm", "head"),
        P("head"),
        P("tm"),
    )
    out_specs = (P("tm", "head"), P("tm", "head"), P("tm", "head"), P("tm", "head"), P("head"))
    return jax.shard_map(body, mesh=mesh, in_specs=in_specs, out_specs=out_specs, check_vma=False)
```

```python
import functools

import jax
import jax.numpy as jnp
from jax import lax
from jax.experimental import pallas as pl
from jax.experimental.pallas import tpu as pltpu
from jax.sharding import PartitionSpec as P

HSZ = 128
BLK = 128
REACH = 4
NEG = -1e30
MESH = pl.DeviceIdType.MESH
F32 = jnp.float32
BF16 = jnp.bfloat16


def nt(a, b):
    return lax.dot_general(a, b, (((1,), (1,)), ((), ())), preferred_element_type=F32)


def tn(a, b):
    return lax.dot_general(a, b, (((0,), (0,)), ((), ())), preferred_element_type=F32)


def nn(a, b):
    return lax.dot_general(a, b, (((1,), (0,)), ((), ())), preferred_element_type=F32)


def radices(count):
    found, stride = [], 1
    while stride < count:
        radix = min(4, count // stride)
        found.append((stride, radix))
        stride *= radix
    return found


def kernel(
    n_tm,
    n_head,
    heads,
    stages,
    q_hbm,
    k_hbm,
    v_hbm,
    g_hbm,
    gain_ref,
    ids_ref,
    normed_ref,
    dq_ref,
    dk_ref,
    dv_ref,
    dgain_ref,
    qb,
    kb,
    vb,
    db,
    q4,
    k4,
    v4,
    d4,
    gb,
    ids_own,
    ids_prev,
    ids_next,
    stats_own,
    stats_next,
    s_ref,
    s4_ref,
    r_ref,
    r4_ref,
    out_acc,
    att_ref,
    sums_own,
    sums_in,
    gain_own,
    gain_in,
    dq_acc,
    dk_acc,
    dv_acc,
    local_sem,
    k_send,
    k_recv,
    q_send,
    q_recv,
    v_send,
    v_recv,
    d_send,
    d_recv,
    ip_send,
    ip_recv,
    in_send,
    in_recv,
    st_send,
    st_recv,
    hd_send,
    hd_recv,
    gn_send,
    gn_recv,
):
    tm = lax.axis_index("tm")
    head = lax.axis_index("head")
    later = (lax.rem(tm + 1, n_tm), head)
    earlier = (lax.rem(tm + n_tm - 1, n_tm), head)
    factor = HSZ ** (-0.5)
    features = HSZ * heads * n_head

    def local(which, src, dst, h):
        return pltpu.make_async_copy(
            src.at[:, h * HSZ : (h + 1) * HSZ], dst.at[h], local_sem.at[which, h]
        )

    loads = []
    for which, (src, dst) in enumerate(
        [(k_hbm, kb.at[0]), (q_hbm, qb.at[0]), (v_hbm, vb.at[0]), (g_hbm, gb)]
    ):
        loads.append([local(which, src, dst, h) for h in range(heads)])
        for one in loads[-1]:
            one.start()

    ids_own[...] = jnp.zeros(ids_own.shape, jnp.int32)
    ids_own[0:1, :] = jnp.full((1, BLK), ids_ref[0], jnp.int32)
    ids_own[1:2, :] = jnp.full((1, BLK), ids_ref[1], jnp.int32)

    def gain_peer(stage, off):
        stride, radix = stages[stage]
        digit = lax.rem(tm // stride, radix)
        return (tm + (lax.rem(digit + off, radix) - digit) * stride, head)

    barrier = pltpu.get_barrier_semaphore()
    greeted = [later, earlier]
    greeted += [(tm, lax.rem(head + off, n_head)) for off in range(1, n_head)]
    for stage, (_, radix) in enumerate(stages):
        greeted += [gain_peer(stage, off) for off in range(1, radix)]
    for peer in greeted:
        pl.semaphore_signal(barrier, inc=1, device_id=peer, device_id_type=MESH)
    pl.semaphore_wait(barrier, len(greeted))

    def remote(src, dst, send, recv, peer):
        return pltpu.make_async_remote_copy(
            src_ref=src,
            dst_ref=dst,
            send_sem=send,
            recv_sem=recv,
            device_id=peer,
            device_id_type=MESH,
        )

    def chain(full, last, send, recv, peer, rows, hop, h):
        if hop < REACH - 1:
            src, dst = full.at[hop, h], full.at[hop + 1, h]
        else:
            src, dst = full.at[hop, h, rows, :], last.at[h]
        return remote(src, dst, send.at[hop, h], recv.at[hop, h], peer)

    low, high = pl.ds(0, BLK), pl.ds(BLK, BLK)
    k_hop = functools.partial(chain, kb, k4, k_send, k_recv, later, high)
    v_hop = functools.partial(chain, vb, v4, v_send, v_recv, later, high)
    q_hop = functools.partial(chain, qb, q4, q_send, q_recv, earlier, low)
    d_hop = functools.partial(chain, db, d4, d_send, d_recv, earlier, low)

    def small_hop(own, got, send, recv, peer, hop):
        src = own if hop == 0 else got.at[hop - 1]
        return remote(src, got.at[hop], send.at[hop], recv.at[hop], peer)

    ip_hop = functools.partial(small_hop, ids_own, ids_prev, ip_send, ip_recv, later)
    in_hop = functools.partial(small_hop, ids_own, ids_next, in_send, in_recv, earlier)
    st_hop = functools.partial(small_hop, stats_own, stats_next, st_send, st_recv, earlier)

    def over_heads(step):
        lax.fori_loop(0, heads, lambda h, c: (step(h), c)[1], 0)

    def bias_row(key_row, query_rows):
        parts = [jnp.where(key_row == row, 0.0, NEG).astype(F32) for row in query_rows]
        return parts[0] if len(parts) == 1 else jnp.concatenate(parts, axis=1)

    ip_hop(0).start()
    in_hop(0).start()
    for h in range(heads):
        loads[0][h].wait()
        k_hop(0, h).start()
        loads[1][h].wait()
        q_hop(0, h).start()

    own_rows = [ids_own[0:1, :], ids_own[1:2, :]]

    def score_block(dst, keys, queries, biases):
        for part in range(2):
            rows = pl.ds(part * BLK, BLK)
            dst[rows, :] = nt(keys[rows, :], queries[...]) * factor + biases[part]

    own_bias = [bias_row(own_rows[p], own_rows) for p in range(2)]
    over_heads(lambda h: score_block(s_ref.at[0, h], kb.at[0, h], qb.at[0, h], own_bias))

    for d in range(1, REACH):
        ip_hop(d - 1).wait_recv()
        ip_hop(d).start()
        in_hop(d - 1).wait_recv()
        in_hop(d).start()
        prev_rows = [ids_prev[d - 1, 0:1, :], ids_prev[d - 1, 1:2, :]]
        next_rows = [ids_next[d - 1, 0:1, :], ids_next[d - 1, 1:2, :]]
        s_bias = [bias_row(prev_rows[p], own_rows) for p in range(2)]
        r_bias = [bias_row(own_rows[p], next_rows) for p in range(2)]

        def arrive(h, d=d, s_bias=s_bias, r_bias=r_bias):
            k_hop(d - 1, h).wait_recv()
            k_hop(d, h).start()
            q_hop(d - 1, h).wait_recv()
            q_hop(d, h).start()
            score_block(s_ref.at[d, h], kb.at[d, h], qb.at[0, h], s_bias)
            score_block(r_ref.at[d - 1, h], kb.at[0, h], qb.at[d, h], r_bias)

        over_heads(arrive)

    for h in range(heads):
        loads[2][h].wait()
        v_hop(0, h).start()
    ip_hop(3).wait_recv()
    in_hop(3).wait_recv()
    s4_bias = bias_row(ids_prev[3, 1:2, :], [own_rows[0]])
    r4_bias = bias_row(own_rows[1], [ids_next[3, 0:1, :]])

    def soften(h):
        k_hop(3, h).wait_recv()
        q_hop(3, h).wait_recv()
        s4 = nt(k4[h], qb[0, h, 0:BLK, :]) * factor + s4_bias
        r4_ref[h] = nt(kb[0, h, BLK : 2 * BLK, :], q4[h]) * factor + r4_bias
        top = jnp.max(s_ref[0, h], axis=0, keepdims=True)
        for d in range(1, REACH):
            top = jnp.maximum(top, jnp.max(s_ref[d, h], axis=0, keepdims=True))
        top4 = jnp.max(s4, axis=0, keepdims=True)
        top_low = jnp.maximum(top[:, 0:BLK], top4)
        top = jnp.concatenate([top_low, top[:, BLK:]], axis=1)
        e4 = jnp.exp(s4 - top_low)
        total4 = jnp.sum(e4, axis=0, keepdims=True)
        total = jnp.concatenate([total4, jnp.zeros((1, BLK), F32)], axis=1)
        for d in range(REACH):
            e = jnp.exp(s_ref[d, h] - top)
            s_ref[d, h] = e
            total = total + jnp.sum(e, axis=0, keepdims=True)
        inverse = 1.0 / total
        for d in range(REACH):
            s_ref[d, h] = s_ref[d, h] * inverse
        s4_ref[h] = e4 * inverse[:, 0:BLK]
        stats_own[pl.ds(h, 1), :] = top + jnp.log(total)
        out_acc[h] = tn(s_ref[0, h].astype(BF16), vb[0, h])

    stats_own[...] = jnp.zeros(stats_own.shape, F32)
    over_heads(soften)

    for d in range(1, REACH):

        def attend(h, d=d):
            v_hop(d - 1, h).wait_recv()
            v_hop(d, h).start()
            out_acc[h] += tn(s_ref[d, h].astype(BF16), vb[d, h])

        over_heads(attend)

    for h in range(heads):
        loads[3][h].wait()
    square = jnp.zeros((2 * BLK, HSZ), F32)
    cross = jnp.zeros((2 * BLK, HSZ), F32)
    for h in range(heads):
        v_hop(3, h).wait_recv()
        out_acc[h, 0:BLK, :] += tn(s4_ref[h].astype(BF16), v4[h])
        att_b = out_acc[h].astype(BF16)
        att_ref[h] = att_b
        att = att_b.astype(F32)
        scaled = gb[h].astype(F32) * gain_ref[h * HSZ : (h + 1) * HSZ].reshape(1, HSZ)
        square = square + att * att
        cross = cross + scaled * att
    sums_own[...] = jnp.zeros(sums_own.shape, F32)
    sums_own[0:1, :] = jnp.sum(square.T, axis=0, keepdims=True)
    sums_own[1:2, :] = jnp.sum(cross.T, axis=0, keepdims=True)

    def head_copy(off):
        return remote(
            sums_own,
            sums_in.at[off - 1],
            hd_send.at[off - 1],
            hd_recv.at[off - 1],
            (tm, lax.rem(head + off, n_head)),
        )

    for off in range(1, n_head):
        head_copy(off).start()
    sums = sums_own[...]
    for off in range(1, n_head):
        head_copy(off).wait_recv()
        sums = sums + sums_in[off - 1]
    rms_row = 1.0 / jnp.sqrt(sums[0:1, :] / features + 1e-06)
    pull_row = rms_row * rms_row * sums[1:2, :] / features
    rms = jnp.broadcast_to(rms_row, (HSZ, 2 * BLK)).T
    pull = jnp.broadcast_to(pull_row, (HSZ, 2 * BLK)).T

    gain_own[...] = jnp.zeros(gain_own.shape, F32)
    for h in range(heads):
        cols = slice(h * HSZ, (h + 1) * HSZ)
        att = att_ref[h].astype(F32)
        grad = gb[h].astype(F32)
        gain = gain_ref[cols].reshape(1, HSZ)
        grad_att = (rms * (grad * gain - att * pull)).astype(BF16)
        db[0, h] = grad_att
        delta = att * grad_att.astype(F32)
        stats_own[heads + h : heads + h + 1, :] = jnp.sum(delta.T, axis=0, keepdims=True)
        d_hop(0, h).start()
        scaled_att = att * rms
        normed_ref[:, cols] = (scaled_att * gain).astype(BF16)
        gain_own[0, h : h + 1, :] = jnp.sum(grad * scaled_att, axis=0, keepdims=True)
    st_hop(0).start()

    def gain_copy(stage, off):
        return remote(
            gain_own.at[stage],
            gain_in.at[stage, off - 1],
            gn_send.at[stage, off - 1],
            gn_recv.at[stage, off - 1],
            gain_peer(stage, off),
        )

    def gain_begin(stage):
        for off in range(1, stages[stage][1]):
            gain_copy(stage, off).start()

    def gain_end(stage):
        total = gain_own[stage]
        for off in range(1, stages[stage][1]):
            gain_copy(stage, off).wait_recv()
            total = total + gain_in[stage, off - 1]
        gain_own[stage + 1] = total

    gain_begin(0)

    def own_block(h):
        weights = s_ref[0, h]
        grad_h = db[0, h]
        delta = stats_own[pl.ds(heads + h, 1), :]
        dscore = (weights * (nt(vb[0, h], grad_h) - delta)).astype(BF16)
        dq_acc[h] = tn(dscore, kb[0, h])
        dk_acc[h] = nn(dscore, qb[0, h])
        dv_acc[h] = nn(weights.astype(BF16), grad_h)

    over_heads(own_block)

    for d in range(1, REACH):
        st_hop(d - 1).wait_recv()
        st_hop(d).start()

        def backward(h, d=d):
            d_hop(d - 1, h).wait_recv()
            d_hop(d, h).start()
            delta = stats_own[pl.ds(heads + h, 1), :]
            dscore = (s_ref[d, h] * (nt(vb[d, h], db[0, h]) - delta)).astype(BF16)
            dq_acc[h] += tn(dscore, kb[d, h])
            log_total = stats_next[d - 1, pl.ds(h, 1), :]
            delta = stats_next[d - 1, pl.ds(heads + h, 1), :]
            weights = jnp.exp(r_ref[d - 1, h] - log_total)
            grad_h = db[d, h]
            dv_acc[h] += nn(weights.astype(BF16), grad_h)
            dscore = (weights * (nt(vb[0, h], grad_h) - delta)).astype(BF16)
            dk_acc[h] += nn(dscore, qb[d, h])

        over_heads(backward)
        if d - 1 < len(stages):
            gain_end(d - 1)
            if d < len(stages):
                gain_begin(d)

    st_hop(3).wait_recv()
    for h in range(heads):
        cols = slice(h * HSZ, (h + 1) * HSZ)
        delta = stats_own[heads + h : heads + h + 1, 0:BLK]
        dscore = (s4_ref[h] * (nt(v4[h], db[0, h, 0:BLK, :]) - delta)).astype(BF16)
        dq_acc[h, 0:BLK, :] += tn(dscore, k4[h])
        dq_ref[:, cols] = (dq_acc[h] * factor).astype(BF16)
    for h in range(heads):
        cols = slice(h * HSZ, (h + 1) * HSZ)
        d_hop(3, h).wait_recv()
        log_total = stats_next[3, h : h + 1, 0:BLK]
        delta = stats_next[3, heads + h : heads + h + 1, 0:BLK]
        weights = jnp.exp(r4_ref[h] - log_total)
        grad_h = d4[h]
        dv_acc[h, BLK : 2 * BLK, :] += nn(weights.astype(BF16), grad_h)
        dscore = (weights * (nt(vb[0, h, BLK : 2 * BLK, :], grad_h) - delta)).astype(BF16)
        dk_acc[h, BLK : 2 * BLK, :] += nn(dscore, q4[h])
        dk_ref[:, cols] = (dk_acc[h] * factor).astype(BF16)
        dv_ref[:, cols] = dv_acc[h].astype(BF16)
        dgain_ref[0:1, cols] = gain_own[len(stages), h : h + 1, :]

    for hop in range(REACH):
        ip_hop(hop).wait_send()
        in_hop(hop).wait_send()
        st_hop(hop).wait_send()
        for h in range(heads):
            k_hop(hop, h).wait_send()
            q_hop(hop, h).wait_send()
            v_hop(hop, h).wait_send()
            d_hop(hop, h).wait_send()
    for off in range(1, n_head):
        head_copy(off).wait_send()
    for stage, (_, radix) in enumerate(stages):
        for off in range(1, radix):
            gain_copy(stage, off).wait_send()


def put_out(*refs):
    ins, outs, sem = refs[:5], refs[5:10], refs[10]
    copies = [pltpu.make_async_copy(ins[i], outs[i], sem.at[i]) for i in range(4)]
    for one in copies:
        one.start()
    for h in range(outs[4].shape[0] // HSZ):
        cols = slice(h * HSZ, (h + 1) * HSZ)
        outs[4][cols] = ins[4][0:1, cols].reshape(HSZ)
    for one in copies:
        one.wait()


def body(queries, key_rows, value_rows, grad_normed, norm_gain, utter_ids):
    rows, width = queries.shape
    heads = width // HSZ
    n_tm, n_head = lax.axis_size("tm"), lax.axis_size("head")
    stages = radices(n_tm)
    full = pltpu.VMEM((REACH, heads, rows, HSZ), BF16)
    last = pltpu.VMEM((heads, BLK, HSZ), BF16)
    wide = pltpu.VMEM((heads, rows, HSZ), F32)
    dma = pltpu.SemaphoreType.DMA
    hops = [dma((REACH, heads))] * 8 + [dma((REACH,))] * 6
    most = max(radix for _, radix in stages) - 1
    scratch = [full] * 4 + [last] * 4
    scratch += [
        pltpu.VMEM((heads, rows, HSZ), BF16),
        pltpu.VMEM((8, BLK), jnp.int32),
        pltpu.VMEM((REACH, 8, BLK), jnp.int32),
        pltpu.VMEM((REACH, 8, BLK), jnp.int32),
        pltpu.VMEM((8, rows), F32),
        pltpu.VMEM((REACH, 8, rows), F32),
        pltpu.VMEM((REACH, heads, rows, rows), F32),
        pltpu.VMEM((heads, BLK, BLK), F32),
        pltpu.VMEM((REACH - 1, heads, rows, rows), F32),
        pltpu.VMEM((heads, BLK, BLK), F32),
        wide,
        pltpu.VMEM((heads, rows, HSZ), BF16),
        pltpu.VMEM((8, rows), F32),
        pltpu.VMEM((n_head - 1, 8, rows), F32),
        pltpu.VMEM((len(stages) + 1, 8, HSZ), F32),
        pltpu.VMEM((len(stages), most, 8, HSZ), F32),
        wide,
        wide,
        wide,
        dma((4, heads)),
    ]
    scratch += hops
    scratch += [dma((n_head - 1,))] * 2 + [dma((len(stages), most))] * 2
    hbm = pl.BlockSpec(memory_space=pl.ANY)
    vmem = pl.BlockSpec(memory_space=pltpu.VMEM)
    big = jax.ShapeDtypeStruct((rows, width), BF16)
    outs = pl.pallas_call(
        functools.partial(kernel, n_tm, n_head, heads, stages),
        out_shape=[big] * 4 + [jax.ShapeDtypeStruct((1, width), F32)],
        in_specs=[hbm] * 4 + [vmem, pl.BlockSpec(memory_space=pltpu.SMEM)],
        out_specs=[vmem] * 5,
        scratch_shapes=scratch,
        compiler_params=pltpu.CompilerParams(collective_id=0, has_side_effects=True),
        name="attention_step",
    )(queries, key_rows, value_rows, grad_normed, norm_gain, utter_ids)
    return tuple(
        pl.pallas_call(
            put_out,
            out_shape=[big] * 4 + [jax.ShapeDtypeStruct((width,), F32)],
            in_specs=[vmem] * 5,
            out_specs=[hbm] * 4 + [vmem],
            scratch_shapes=[dma((4,))],
            name="put_out",
        )(*outs)
    )


def solution(mesh):
    in_specs = (
        P("tm", "head"),
        P("tm", "head"),
        P("tm", "head"),
        P("tm", "head"),
        P("head"),
        P("tm"),
    )
    out_specs = (P("tm", "head"), P("tm", "head"), P("tm", "head"), P("tm", "head"), P("head"))
    return jax.shard_map(body, mesh=mesh, in_specs=in_specs, out_specs=out_specs, check_vma=False)
```

```python
import functools

import jax
import jax.numpy as jnp
from jax import lax
from jax.experimental import pallas as pl
from jax.experimental.pallas import tpu as pltpu
from jax.sharding import PartitionSpec as P

HSZ = 128
BLK = 128
REACH = 4
NEG = -1e30
MESH = pl.DeviceIdType.MESH
F32 = jnp.float32
BF16 = jnp.bfloat16


def nt(a, b):
    return lax.dot_general(a, b, (((1,), (1,)), ((), ())), preferred_element_type=F32)


def tn(a, b):
    return lax.dot_general(a, b, (((0,), (0,)), ((), ())), preferred_element_type=F32)


def nn(a, b):
    return lax.dot_general(a, b, (((1,), (0,)), ((), ())), preferred_element_type=F32)


def radices(count):
    found, stride = [], 1
    while stride < count:
        radix = min(4, count // stride)
        found.append((stride, radix))
        stride *= radix
    return found


def kernel(
    n_tm,
    n_head,
    heads,
    stages,
    q_hbm,
    k_hbm,
    v_hbm,
    g_hbm,
    gain_ref,
    ids_ref,
    normed_ref,
    dq_ref,
    dk_ref,
    dv_ref,
    dgain_ref,
    qb,
    kb,
    vb,
    gb,
    ab,
    q4,
    k4,
    v4,
    g4,
    a4,
    db,
    ids_own,
    ids_prev,
    ids_next,
    stats_own,
    stats_next,
    s_ref,
    s4_ref,
    r_ref,
    r4_ref,
    out_acc,
    sums_own,
    sums_in,
    gain_own,
    gain_in,
    dq_acc,
    dk_acc,
    dv_acc,
    gain_rows,
    rms_d,
    pull_d,
    local_sem,
    k_send,
    k_recv,
    q_send,
    q_recv,
    v_send,
    v_recv,
    g_send,
    g_recv,
    a_send,
    a_recv,
    ip_send,
    ip_recv,
    in_send,
    in_recv,
    st_send,
    st_recv,
    hd_send,
    hd_recv,
    gn_send,
    gn_recv,
):
    tm = lax.axis_index("tm")
    head = lax.axis_index("head")
    later = (lax.rem(tm + 1, n_tm), head)
    earlier = (lax.rem(tm + n_tm - 1, n_tm), head)
    factor = HSZ ** (-0.5)
    features = HSZ * heads * n_head

    def local(which, src, dst, h):
        return pltpu.make_async_copy(
            src.at[:, h * HSZ : (h + 1) * HSZ], dst.at[h], local_sem.at[which, h]
        )

    loads = []
    for which, (src, dst) in enumerate(
        [(k_hbm, kb.at[0]), (q_hbm, qb.at[0]), (v_hbm, vb.at[0]), (g_hbm, gb.at[0])]
    ):
        loads.append([local(which, src, dst, h) for h in range(heads)])
        for one in loads[-1]:
            one.start()

    ids_own[...] = jnp.zeros(ids_own.shape, jnp.int32)
    ids_own[0:1, :] = jnp.full((1, BLK), ids_ref[0], jnp.int32)
    ids_own[1:2, :] = jnp.full((1, BLK), ids_ref[1], jnp.int32)

    def gain_peer(stage, off):
        stride, radix = stages[stage]
        digit = lax.rem(tm // stride, radix)
        return (tm + (lax.rem(digit + off, radix) - digit) * stride, head)

    barrier = pltpu.get_barrier_semaphore()
    greeted = [later, earlier]
    greeted += [(tm, lax.rem(head + off, n_head)) for off in range(1, n_head)]
    for stage, (_, radix) in enumerate(stages):
        greeted += [gain_peer(stage, off) for off in range(1, radix)]
    for peer in greeted:
        pl.semaphore_signal(barrier, inc=1, device_id=peer, device_id_type=MESH)
    pl.semaphore_wait(barrier, len(greeted))

    def remote(src, dst, send, recv, peer):
        return pltpu.make_async_remote_copy(
            src_ref=src,
            dst_ref=dst,
            send_sem=send,
            recv_sem=recv,
            device_id=peer,
            device_id_type=MESH,
        )

    def chain(full, last, send, recv, peer, rows, hop, h):
        if hop < REACH - 1:
            src, dst = full.at[hop, h], full.at[hop + 1, h]
        else:
            src, dst = full.at[hop, h, rows, :], last.at[h]
        return remote(src, dst, send.at[hop, h], recv.at[hop, h], peer)

    low, high = pl.ds(0, BLK), pl.ds(BLK, BLK)
    k_hop = functools.partial(chain, kb, k4, k_send, k_recv, later, high)
    v_hop = functools.partial(chain, vb, v4, v_send, v_recv, later, high)
    q_hop = functools.partial(chain, qb, q4, q_send, q_recv, earlier, low)
    g_hop = functools.partial(chain, gb, g4, g_send, g_recv, earlier, low)
    a_hop = functools.partial(chain, ab, a4, a_send, a_recv, earlier, low)

    def small_hop(own, got, send, recv, peer, hop):
        src = own if hop == 0 else got.at[hop - 1]
        return remote(src, got.at[hop], send.at[hop], recv.at[hop], peer)

    ip_hop = functools.partial(small_hop, ids_own, ids_prev, ip_send, ip_recv, later)
    in_hop = functools.partial(small_hop, ids_own, ids_next, in_send, in_recv, earlier)
    st_hop = functools.partial(small_hop, stats_own, stats_next, st_send, st_recv, earlier)

    def over_heads(step):
        lax.fori_loop(0, heads, lambda h, c: (step(h), c)[1], 0)

    def bias_row(key_row, query_rows):
        parts = [jnp.where(key_row == row, 0.0, NEG).astype(F32) for row in query_rows]
        return parts[0] if len(parts) == 1 else jnp.concatenate(parts, axis=1)

    ip_hop(0).start()
    in_hop(0).start()
    for h in range(heads):
        loads[0][h].wait()
        k_hop(0, h).start()
        loads[1][h].wait()
        q_hop(0, h).start()

    own_rows = [ids_own[0:1, :], ids_own[1:2, :]]

    def score_block(dst, keys, queries, biases):
        for part in range(2):
            rows = pl.ds(part * BLK, BLK)
            dst[rows, :] = nt(keys[rows, :], queries[...]) * factor + biases[part]

    own_bias = [bias_row(own_rows[p], own_rows) for p in range(2)]
    over_heads(lambda h: score_block(s_ref.at[0, h], kb.at[0, h], qb.at[0, h], own_bias))

    for d in range(1, REACH):
        ip_hop(d - 1).wait_recv()
        ip_hop(d).start()
        in_hop(d - 1).wait_recv()
        in_hop(d).start()
        prev_rows = [ids_prev[d - 1, 0:1, :], ids_prev[d - 1, 1:2, :]]
        next_rows = [ids_next[d - 1, 0:1, :], ids_next[d - 1, 1:2, :]]
        s_bias = [bias_row(prev_rows[p], own_rows) for p in range(2)]
        r_bias = [bias_row(own_rows[p], next_rows) for p in range(2)]

        def arrive(h, d=d, s_bias=s_bias, r_bias=r_bias):
            k_hop(d - 1, h).wait_recv()
            k_hop(d, h).start()
            q_hop(d - 1, h).wait_recv()
            q_hop(d, h).start()
            score_block(s_ref.at[d, h], kb.at[d, h], qb.at[0, h], s_bias)
            score_block(r_ref.at[d - 1, h], kb.at[0, h], qb.at[d, h], r_bias)

        over_heads(arrive)

    for h in range(heads):
        loads[2][h].wait()
        v_hop(0, h).start()
        loads[3][h].wait()
        g_hop(0, h).start()
    ip_hop(3).wait_recv()
    in_hop(3).wait_recv()
    s4_bias = bias_row(ids_prev[3, 1:2, :], [own_rows[0]])
    r4_bias = bias_row(own_rows[1], [ids_next[3, 0:1, :]])

    def soften(h):
        k_hop(3, h).wait_recv()
        q_hop(3, h).wait_recv()
        s4 = nt(k4[h], qb[0, h, 0:BLK, :]) * factor + s4_bias
        r4_ref[h] = nt(kb[0, h, BLK : 2 * BLK, :], q4[h]) * factor + r4_bias
        top = jnp.max(s_ref[0, h], axis=0, keepdims=True)
        for d in range(1, REACH):
            top = jnp.maximum(top, jnp.max(s_ref[d, h], axis=0, keepdims=True))
        top4 = jnp.max(s4, axis=0, keepdims=True)
        top_low = jnp.maximum(top[:, 0:BLK], top4)
        top = jnp.concatenate([top_low, top[:, BLK:]], axis=1)
        e4 = jnp.exp(s4 - top_low)
        total4 = jnp.sum(e4, axis=0, keepdims=True)
        total = jnp.concatenate([total4, jnp.zeros((1, BLK), F32)], axis=1)
        for d in range(REACH):
            e = jnp.exp(s_ref[d, h] - top)
            s_ref[d, h] = e
            total = total + jnp.sum(e, axis=0, keepdims=True)
        inverse = 1.0 / total
        for d in range(REACH):
            s_ref[d, h] = s_ref[d, h] * inverse
        s4_ref[h] = e4 * inverse[:, 0:BLK]
        stats_own[pl.ds(h, 1), :] = top + jnp.log(total)
        out_acc[h] = tn(s_ref[0, h].astype(BF16), vb[0, h])

    stats_own[...] = jnp.zeros(stats_own.shape, F32)
    over_heads(soften)

    for d in range(1, REACH):

        def attend(h, d=d):
            v_hop(d - 1, h).wait_recv()
            v_hop(d, h).start()
            g_hop(d - 1, h).wait_recv()
            g_hop(d, h).start()
            out_acc[h] += tn(s_ref[d, h].astype(BF16), vb[d, h])

        over_heads(attend)

    square = jnp.zeros((2 * BLK, HSZ), F32)
    cross = jnp.zeros((2 * BLK, HSZ), F32)
    for h in range(heads):
        v_hop(3, h).wait_recv()
        out_acc[h, 0:BLK, :] += tn(s4_ref[h].astype(BF16), v4[h])
        att_b = out_acc[h].astype(BF16)
        ab[0, h] = att_b
        att = att_b.astype(F32)
        scaled = gb[0, h].astype(F32) * gain_ref[h * HSZ : (h + 1) * HSZ].reshape(1, HSZ)
        square = square + att * att
        cross = cross + scaled * att
        a_hop(0, h).start()
    sums_own[...] = jnp.zeros(sums_own.shape, F32)
    sums_own[0:1, :] = jnp.sum(square.T, axis=0, keepdims=True)
    sums_own[1:2, :] = jnp.sum(cross.T, axis=0, keepdims=True)

    def head_copy(off):
        return remote(
            sums_own,
            sums_in.at[off - 1],
            hd_send.at[off - 1],
            hd_recv.at[off - 1],
            (tm, lax.rem(head + off, n_head)),
        )

    for off in range(1, n_head):
        head_copy(off).start()
    sums = sums_own[...]
    for off in range(1, n_head):
        head_copy(off).wait_recv()
        sums = sums + sums_in[off - 1]
    rms_row = 1.0 / jnp.sqrt(sums[0:1, :] / features + 1e-06)
    pull_row = rms_row * rms_row * sums[1:2, :] / features
    stats_own[2 * heads : 2 * heads + 1, :] = rms_row
    stats_own[2 * heads + 1 : 2 * heads + 2, :] = pull_row

    def column(row, count):
        return jnp.broadcast_to(row, (HSZ, count)).T

    def cotangent(att_b, grad_b, gain, rms, pull):
        return (rms * (grad_b.astype(F32) * gain - att_b.astype(F32) * pull)).astype(BF16)

    rms = column(rms_row, 2 * BLK)
    pull = column(pull_row, 2 * BLK)
    for h in range(heads):
        gain = gain_ref[h * HSZ : (h + 1) * HSZ].reshape(1, HSZ)
        att_b = ab[0, h]
        grad_att = cotangent(att_b, gb[0, h], gain, rms, pull)
        db[h] = grad_att
        delta = att_b.astype(F32) * grad_att.astype(F32)
        stats_own[heads + h : heads + h + 1, :] = jnp.sum(delta.T, axis=0, keepdims=True)
    st_hop(0).start()
    gain_own[...] = jnp.zeros(gain_own.shape, F32)
    for h in range(heads):
        a_hop(0, h).wait_recv()
        a_hop(1, h).start()
        cols = slice(h * HSZ, (h + 1) * HSZ)
        scaled_att = ab[0, h].astype(F32) * rms
        normed_ref[:, cols] = (scaled_att * gain_ref[cols].reshape(1, HSZ)).astype(BF16)
        gain_own[0, h : h + 1, :] = jnp.sum(
            gb[0, h].astype(F32) * scaled_att, axis=0, keepdims=True
        )

    def gain_copy(stage, off):
        return remote(
            gain_own.at[stage],
            gain_in.at[stage, off - 1],
            gn_send.at[stage, off - 1],
            gn_recv.at[stage, off - 1],
            gain_peer(stage, off),
        )

    def gain_begin(stage):
        for off in range(1, stages[stage][1]):
            gain_copy(stage, off).start()

    def gain_end(stage):
        total = gain_own[stage]
        for off in range(1, stages[stage][1]):
            gain_copy(stage, off).wait_recv()
            total = total + gain_in[stage, off - 1]
        gain_own[stage + 1] = total

    gain_begin(0)

    def own_block(h):
        a_hop(1, h).wait_recv()
        a_hop(2, h).start()
        weights = s_ref[0, h]
        grad_h = db[h]
        delta = stats_own[pl.ds(heads + h, 1), :]
        dscore = (weights * (nt(vb[0, h], grad_h) - delta)).astype(BF16)
        dq_acc[h] = tn(dscore, kb[0, h])
        dk_acc[h] = nn(dscore, qb[0, h])
        dv_acc[h] = nn(weights.astype(BF16), grad_h)

    over_heads(own_block)

    for h in range(heads):
        cols = slice(h * HSZ, (h + 1) * HSZ)
        gain_rows[h] = jnp.broadcast_to(gain_ref[cols].reshape(1, HSZ), (8, HSZ))

    for d in range(1, REACH):
        st_hop(d - 1).wait_recv()
        st_hop(d).start()
        rms_d[...] = column(stats_next[d - 1, 2 * heads : 2 * heads + 1, :], 2 * BLK)
        pull_d[...] = column(stats_next[d - 1, 2 * heads + 1 : 2 * heads + 2, :], 2 * BLK)

        def backward(h, d=d):
            if d == 1:
                a_hop(2, h).wait_recv()
                a_hop(3, h).start()
            delta = stats_own[pl.ds(heads + h, 1), :]
            dscore = (s_ref[d, h] * (nt(vb[d, h], db[h]) - delta)).astype(BF16)
            dq_acc[h] += tn(dscore, kb[d, h])
            grad_h = cotangent(
                ab[d, h], gb[d, h], gain_rows[h, 0:1, :], rms_d[...], pull_d[...]
            )
            log_total = stats_next[d - 1, pl.ds(h, 1), :]
            delta = stats_next[d - 1, pl.ds(heads + h, 1), :]
            weights = jnp.exp(r_ref[d - 1, h] - log_total)
            dv_acc[h] += nn(weights.astype(BF16), grad_h)
            dscore = (weights * (nt(vb[0, h], grad_h) - delta)).astype(BF16)
            dk_acc[h] += nn(dscore, qb[d, h])

        over_heads(backward)
        if d - 1 < len(stages):
            gain_end(d - 1)
            if d < len(stages):
                gain_begin(d)

    st_hop(3).wait_recv()
    for h in range(heads):
        cols = slice(h * HSZ, (h + 1) * HSZ)
        delta = stats_own[heads + h : heads + h + 1, 0:BLK]
        dscore = (s4_ref[h] * (nt(v4[h], db[h, 0:BLK, :]) - delta)).astype(BF16)
        dq_acc[h, 0:BLK, :] += tn(dscore, k4[h])
        dq_ref[:, cols] = (dq_acc[h] * factor).astype(BF16)
    rms = column(stats_next[3, 2 * heads : 2 * heads + 1, 0:BLK], BLK)
    pull = column(stats_next[3, 2 * heads + 1 : 2 * heads + 2, 0:BLK], BLK)
    for h in range(heads):
        cols = slice(h * HSZ, (h + 1) * HSZ)
        g_hop(3, h).wait_recv()
        a_hop(3, h).wait_recv()
        log_total = stats_next[3, h : h + 1, 0:BLK]
        delta = stats_next[3, heads + h : heads + h + 1, 0:BLK]
        weights = jnp.exp(r4_ref[h] - log_total)
        grad_h = cotangent(a4[h], g4[h], gain_rows[h, 0:1, :], rms, pull)
        dv_acc[h, BLK : 2 * BLK, :] += nn(weights.astype(BF16), grad_h)
        dscore = (weights * (nt(vb[0, h, BLK : 2 * BLK, :], grad_h) - delta)).astype(BF16)
        dk_acc[h, BLK : 2 * BLK, :] += nn(dscore, q4[h])
        dk_ref[:, cols] = (dk_acc[h] * factor).astype(BF16)
        dv_ref[:, cols] = dv_acc[h].astype(BF16)
        dgain_ref[0:1, cols] = gain_own[len(stages), h : h + 1, :]

    for hop in range(REACH):
        ip_hop(hop).wait_send()
        in_hop(hop).wait_send()
        st_hop(hop).wait_send()
        for h in range(heads):
            k_hop(hop, h).wait_send()
            q_hop(hop, h).wait_send()
            v_hop(hop, h).wait_send()
            g_hop(hop, h).wait_send()
            a_hop(hop, h).wait_send()
    for off in range(1, n_head):
        head_copy(off).wait_send()
    for stage, (_, radix) in enumerate(stages):
        for off in range(1, radix):
            gain_copy(stage, off).wait_send()


def put_out(*refs):
    ins, outs, sem = refs[:5], refs[5:10], refs[10]
    copies = [pltpu.make_async_copy(ins[i], outs[i], sem.at[i]) for i in range(4)]
    for one in copies:
        one.start()
    for h in range(outs[4].shape[0] // HSZ):
        cols = slice(h * HSZ, (h + 1) * HSZ)
        outs[4][cols] = ins[4][0:1, cols].reshape(HSZ)
    for one in copies:
        one.wait()


def body(queries, key_rows, value_rows, grad_normed, norm_gain, utter_ids):
    rows, width = queries.shape
    heads = width // HSZ
    n_tm, n_head = lax.axis_size("tm"), lax.axis_size("head")
    stages = radices(n_tm)
    full = pltpu.VMEM((REACH, heads, rows, HSZ), BF16)
    last = pltpu.VMEM((heads, BLK, HSZ), BF16)
    wide = pltpu.VMEM((heads, rows, HSZ), F32)
    dma = pltpu.SemaphoreType.DMA
    hops = [dma((REACH, heads))] * 10 + [dma((REACH,))] * 6
    most = max(radix for _, radix in stages) - 1
    scratch = [full] * 5 + [last] * 5
    scratch += [
        pltpu.VMEM((heads, rows, HSZ), BF16),
        pltpu.VMEM((8, BLK), jnp.int32),
        pltpu.VMEM((REACH, 8, BLK), jnp.int32),
        pltpu.VMEM((REACH, 8, BLK), jnp.int32),
        pltpu.VMEM((8, rows), F32),
        pltpu.VMEM((REACH, 8, rows), F32),
        pltpu.VMEM((REACH, heads, rows, rows), F32),
        pltpu.VMEM((heads, BLK, BLK), F32),
        pltpu.VMEM((REACH - 1, heads, rows, rows), F32),
        pltpu.VMEM((heads, BLK, BLK), F32),
        wide,
        pltpu.VMEM((8, rows), F32),
        pltpu.VMEM((n_head - 1, 8, rows), F32),
        pltpu.VMEM((len(stages) + 1, 8, HSZ), F32),
        pltpu.VMEM((len(stages), most, 8, HSZ), F32),
        wide,
        wide,
        wide,
        pltpu.VMEM((heads, 8, HSZ), F32),
        pltpu.VMEM((rows, HSZ), F32),
        pltpu.VMEM((rows, HSZ), F32),
        dma((4, heads)),
    ]
    scratch += hops
    scratch += [dma((n_head - 1,))] * 2 + [dma((len(stages), most))] * 2
    hbm = pl.BlockSpec(memory_space=pl.ANY)
    vmem = pl.BlockSpec(memory_space=pltpu.VMEM)
    big = jax.ShapeDtypeStruct((rows, width), BF16)
    outs = pl.pallas_call(
        functools.partial(kernel, n_tm, n_head, heads, stages),
        out_shape=[big] * 4 + [jax.ShapeDtypeStruct((1, width), F32)],
        in_specs=[hbm] * 4 + [vmem, pl.BlockSpec(memory_space=pltpu.SMEM)],
        out_specs=[vmem] * 5,
        scratch_shapes=scratch,
        compiler_params=pltpu.CompilerParams(collective_id=0, has_side_effects=True),
        name="attention_step",
    )(queries, key_rows, value_rows, grad_normed, norm_gain, utter_ids)
    return tuple(
        pl.pallas_call(
            put_out,
            out_shape=[big] * 4 + [jax.ShapeDtypeStruct((width,), F32)],
            in_specs=[vmem] * 5,
            out_specs=[hbm] * 4 + [vmem],
            scratch_shapes=[dma((4,))],
            name="put_out",
        )(*outs)
    )


def solution(mesh):
    in_specs = (
        P("tm", "head"),
        P("tm", "head"),
        P("tm", "head"),
        P("tm", "head"),
        P("head"),
        P("tm"),
    )
    out_specs = (P("tm", "head"), P("tm", "head"), P("tm", "head"), P("tm", "head"), P("head"))
    return jax.shard_map(body, mesh=mesh, in_specs=in_specs, out_specs=out_specs, check_vma=False)
```

```python
import functools

import jax
import jax.numpy as jnp
from jax import lax
from jax.experimental import pallas as pl
from jax.experimental.pallas import tpu as pltpu
from jax.sharding import PartitionSpec as P

HSZ = 128
BLK = 128
REACH = 4
NEG = -1e30
MESH = pl.DeviceIdType.MESH
F32 = jnp.float32
BF16 = jnp.bfloat16


def nt(a, b):
    return lax.dot_general(a, b, (((1,), (1,)), ((), ())), preferred_element_type=F32)


def tn(a, b):
    return lax.dot_general(a, b, (((0,), (0,)), ((), ())), preferred_element_type=F32)


def nn(a, b):
    return lax.dot_general(a, b, (((1,), (0,)), ((), ())), preferred_element_type=F32)


def radices(count):
    found, stride = [], 1
    while stride < count:
        radix = min(4, count // stride)
        found.append((stride, radix))
        stride *= radix
    return found


def kernel(
    n_tm,
    n_head,
    heads,
    stages,
    q_hbm,
    k_hbm,
    v_hbm,
    g_hbm,
    gain_ref,
    ids_ref,
    normed_ref,
    dq_ref,
    dk_ref,
    dv_ref,
    dgain_ref,
    qb,
    kb,
    vb,
    gb,
    ab,
    q4,
    k4,
    v4,
    g4,
    a4,
    db,
    ids_own,
    ids_prev,
    ids_next,
    stats_own,
    stats_next,
    s_ref,
    s4_ref,
    r_ref,
    r4_ref,
    out_acc,
    sums_own,
    sums_in,
    gain_own,
    gain_in,
    dq_acc,
    dk_acc,
    dv_acc,
    gain_rows,
    rms_d,
    pull_d,
    local_sem,
    k_send,
    k_recv,
    q_send,
    q_recv,
    v_send,
    v_recv,
    g_send,
    g_recv,
    a_send,
    a_recv,
    ip_send,
    ip_recv,
    in_send,
    in_recv,
    st_send,
    st_recv,
    hd_send,
    hd_recv,
    gn_send,
    gn_recv,
):
    tm = lax.axis_index("tm")
    head = lax.axis_index("head")
    later = (lax.rem(tm + 1, n_tm), head)
    earlier = (lax.rem(tm + n_tm - 1, n_tm), head)
    factor = HSZ ** (-0.5)
    features = HSZ * heads * n_head

    def local(which, src, dst, h):
        return pltpu.make_async_copy(
            src.at[:, h * HSZ : (h + 1) * HSZ], dst.at[h], local_sem.at[which, h]
        )

    loads = []
    for which, (src, dst) in enumerate(
        [(k_hbm, kb.at[0]), (q_hbm, qb.at[0]), (v_hbm, vb.at[0]), (g_hbm, gb.at[0])]
    ):
        loads.append([local(which, src, dst, h) for h in range(heads)])
        for one in loads[-1]:
            one.start()

    ids_own[...] = jnp.zeros(ids_own.shape, jnp.int32)
    ids_own[0:1, :] = jnp.full((1, BLK), ids_ref[0], jnp.int32)
    ids_own[1:2, :] = jnp.full((1, BLK), ids_ref[1], jnp.int32)

    def gain_peer(stage, off):
        stride, radix = stages[stage]
        digit = lax.rem(tm // stride, radix)
        return (tm + (lax.rem(digit + off, radix) - digit) * stride, head)

    barrier = pltpu.get_barrier_semaphore()
    greeted = [later, earlier]
    greeted += [(tm, lax.rem(head + off, n_head)) for off in range(1, n_head)]
    for stage, (_, radix) in enumerate(stages):
        greeted += [gain_peer(stage, off) for off in range(1, radix)]
    for peer in greeted:
        pl.semaphore_signal(barrier, inc=1, device_id=peer, device_id_type=MESH)
    pl.semaphore_wait(barrier, len(greeted))

    def remote(src, dst, send, recv, peer):
        return pltpu.make_async_remote_copy(
            src_ref=src,
            dst_ref=dst,
            send_sem=send,
            recv_sem=recv,
            device_id=peer,
            device_id_type=MESH,
        )

    def chain(full, last, send, recv, peer, rows, hop, h):
        if hop < REACH - 1:
            src, dst = full.at[hop, h], full.at[hop + 1, h]
        else:
            src, dst = full.at[hop, h, rows, :], last.at[h]
        return remote(src, dst, send.at[hop, h], recv.at[hop, h], peer)

    low, high = pl.ds(0, BLK), pl.ds(BLK, BLK)
    k_hop = functools.partial(chain, kb, k4, k_send, k_recv, later, high)
    v_hop = functools.partial(chain, vb, v4, v_send, v_recv, later, high)
    q_hop = functools.partial(chain, qb, q4, q_send, q_recv, earlier, low)
    g_hop = functools.partial(chain, gb, g4, g_send, g_recv, earlier, low)
    a_hop = functools.partial(chain, ab, a4, a_send, a_recv, earlier, low)

    def small_hop(own, got, send, recv, peer, hop):
        src = own if hop == 0 else got.at[hop - 1]
        return remote(src, got.at[hop], send.at[hop], recv.at[hop], peer)

    ip_hop = functools.partial(small_hop, ids_own, ids_prev, ip_send, ip_recv, later)
    in_hop = functools.partial(small_hop, ids_own, ids_next, in_send, in_recv, earlier)
    st_hop = functools.partial(small_hop, stats_own, stats_next, st_send, st_recv, earlier)

    def over_heads(step):
        lax.fori_loop(0, heads, lambda h, c: (step(h), c)[1], 0)

    def bias_row(key_row, query_rows):
        parts = [jnp.where(key_row == row, 0.0, NEG).astype(F32) for row in query_rows]
        return parts[0] if len(parts) == 1 else jnp.concatenate(parts, axis=1)

    ip_hop(0).start()
    in_hop(0).start()
    for h in range(heads):
        loads[0][h].wait()
        k_hop(0, h).start()
        loads[1][h].wait()
        q_hop(0, h).start()

    own_rows = [ids_own[0:1, :], ids_own[1:2, :]]

    def score_block(dst, keys, queries, biases):
        for part in range(2):
            rows = pl.ds(part * BLK, BLK)
            dst[rows, :] = nt(keys[rows, :], queries[...]) * factor + biases[part]

    own_bias = [bias_row(own_rows[p], own_rows) for p in range(2)]
    over_heads(lambda h: score_block(s_ref.at[0, h], kb.at[0, h], qb.at[0, h], own_bias))

    for d in range(1, REACH):
        ip_hop(d - 1).wait_recv()
        ip_hop(d).start()
        in_hop(d - 1).wait_recv()
        in_hop(d).start()
        prev_rows = [ids_prev[d - 1, 0:1, :], ids_prev[d - 1, 1:2, :]]
        next_rows = [ids_next[d - 1, 0:1, :], ids_next[d - 1, 1:2, :]]
        s_bias = [bias_row(prev_rows[p], own_rows) for p in range(2)]
        r_bias = [bias_row(own_rows[p], next_rows) for p in range(2)]

        def arrive(h, d=d, s_bias=s_bias, r_bias=r_bias):
            k_hop(d - 1, h).wait_recv()
            k_hop(d, h).start()
            q_hop(d - 1, h).wait_recv()
            q_hop(d, h).start()
            score_block(s_ref.at[d, h], kb.at[d, h], qb.at[0, h], s_bias)
            score_block(r_ref.at[d - 1, h], kb.at[0, h], qb.at[d, h], r_bias)

        over_heads(arrive)

    for h in range(heads):
        loads[2][h].wait()
        v_hop(0, h).start()
        loads[3][h].wait()
        g_hop(0, h).start()
    ip_hop(3).wait_recv()
    in_hop(3).wait_recv()
    s4_bias = bias_row(ids_prev[3, 1:2, :], [own_rows[0]])
    r4_bias = bias_row(own_rows[1], [ids_next[3, 0:1, :]])

    def soften(h):
        k_hop(3, h).wait_recv()
        q_hop(3, h).wait_recv()
        s4 = nt(k4[h], qb[0, h, 0:BLK, :]) * factor + s4_bias
        r4_ref[h] = nt(kb[0, h, BLK : 2 * BLK, :], q4[h]) * factor + r4_bias
        top = jnp.max(s_ref[0, h], axis=0, keepdims=True)
        for d in range(1, REACH):
            top = jnp.maximum(top, jnp.max(s_ref[d, h], axis=0, keepdims=True))
        top4 = jnp.max(s4, axis=0, keepdims=True)
        top_low = jnp.maximum(top[:, 0:BLK], top4)
        top = jnp.concatenate([top_low, top[:, BLK:]], axis=1)
        e4 = jnp.exp(s4 - top_low)
        total4 = jnp.sum(e4, axis=0, keepdims=True)
        total = jnp.concatenate([total4, jnp.zeros((1, BLK), F32)], axis=1)
        for d in range(REACH):
            e = jnp.exp(s_ref[d, h] - top)
            s_ref[d, h] = e
            total = total + jnp.sum(e, axis=0, keepdims=True)
        inverse = 1.0 / total
        for d in range(REACH):
            s_ref[d, h] = s_ref[d, h] * inverse
        s4_ref[h] = e4 * inverse[:, 0:BLK]
        stats_own[pl.ds(h, 1), :] = top + jnp.log(total)
        out_acc[h] = tn(s_ref[0, h].astype(BF16), vb[0, h])

    stats_own[...] = jnp.zeros(stats_own.shape, F32)
    over_heads(soften)

    for d in range(1, REACH):

        def attend(h, d=d):
            v_hop(d - 1, h).wait_recv()
            v_hop(d, h).start()
            g_hop(d - 1, h).wait_recv()
            g_hop(d, h).start()
            out_acc[h] += tn(s_ref[d, h].astype(BF16), vb[d, h])

        over_heads(attend)

    square = jnp.zeros((2 * BLK, HSZ), F32)
    cross = jnp.zeros((2 * BLK, HSZ), F32)
    for h in range(heads):
        v_hop(3, h).wait_recv()
        out_acc[h, 0:BLK, :] += tn(s4_ref[h].astype(BF16), v4[h])
        att_b = out_acc[h].astype(BF16)
        ab[0, h] = att_b
        att = att_b.astype(F32)
        scaled = gb[0, h].astype(F32) * gain_ref[h * HSZ : (h + 1) * HSZ].reshape(1, HSZ)
        square = square + att * att
        cross = cross + scaled * att
        a_hop(0, h).start()
    sums_own[...] = jnp.zeros(sums_own.shape, F32)
    sums_own[0:1, :] = jnp.sum(square.T, axis=0, keepdims=True)
    sums_own[1:2, :] = jnp.sum(cross.T, axis=0, keepdims=True)

    def head_copy(off):
        return remote(
            sums_own,
            sums_in.at[off - 1],
            hd_send.at[off - 1],
            hd_recv.at[off - 1],
            (tm, lax.rem(head + off, n_head)),
        )

    for off in range(1, n_head):
        head_copy(off).start()
    for h in range(heads):
        a_hop(0, h).wait_recv()
        a_hop(1, h).start()
    sums = sums_own[...]
    for off in range(1, n_head):
        head_copy(off).wait_recv()
        sums = sums + sums_in[off - 1]
    rms_row = 1.0 / jnp.sqrt(sums[0:1, :] / features + 1e-06)
    pull_row = rms_row * rms_row * sums[1:2, :] / features
    stats_own[2 * heads : 2 * heads + 1, :] = rms_row
    stats_own[2 * heads + 1 : 2 * heads + 2, :] = pull_row

    def column(row, count):
        return jnp.broadcast_to(row, (HSZ, count)).T

    def cotangent(att_b, grad_b, gain, rms, pull):
        return (rms * (grad_b.astype(F32) * gain - att_b.astype(F32) * pull)).astype(BF16)

    rms = column(rms_row, 2 * BLK)
    pull = column(pull_row, 2 * BLK)
    for h in range(heads):
        gain = gain_ref[h * HSZ : (h + 1) * HSZ].reshape(1, HSZ)
        att_b = ab[0, h]
        grad_att = cotangent(att_b, gb[0, h], gain, rms, pull)
        db[h] = grad_att
        delta = att_b.astype(F32) * grad_att.astype(F32)
        stats_own[heads + h : heads + h + 1, :] = jnp.sum(delta.T, axis=0, keepdims=True)
    st_hop(0).start()
    gain_own[...] = jnp.zeros(gain_own.shape, F32)
    for h in range(heads):
        a_hop(1, h).wait_recv()
        a_hop(2, h).start()
        cols = slice(h * HSZ, (h + 1) * HSZ)
        scaled_att = ab[0, h].astype(F32) * rms
        normed_ref[:, cols] = (scaled_att * gain_ref[cols].reshape(1, HSZ)).astype(BF16)
        gain_own[0, h : h + 1, :] = jnp.sum(
            gb[0, h].astype(F32) * scaled_att, axis=0, keepdims=True
        )

    def gain_copy(stage, off):
        return remote(
            gain_own.at[stage],
            gain_in.at[stage, off - 1],
            gn_send.at[stage, off - 1],
            gn_recv.at[stage, off - 1],
            gain_peer(stage, off),
        )

    def gain_begin(stage):
        for off in range(1, stages[stage][1]):
            gain_copy(stage, off).start()

    def gain_end(stage):
        total = gain_own[stage]
        for off in range(1, stages[stage][1]):
            gain_copy(stage, off).wait_recv()
            total = total + gain_in[stage, off - 1]
        gain_own[stage + 1] = total

    gain_begin(0)

    def own_block(h):
        weights = s_ref[0, h]
        grad_h = db[h]
        delta = stats_own[pl.ds(heads + h, 1), :]
        dscore = (weights * (nt(vb[0, h], grad_h) - delta)).astype(BF16)
        dq_acc[h] = tn(dscore, kb[0, h])
        dk_acc[h] = nn(dscore, qb[0, h])
        dv_acc[h] = nn(weights.astype(BF16), grad_h)

    over_heads(own_block)
    for h in range(heads):
        a_hop(2, h).wait_recv()
        a_hop(3, h).start()

    for h in range(heads):
        cols = slice(h * HSZ, (h + 1) * HSZ)
        gain_rows[h] = jnp.broadcast_to(gain_ref[cols].reshape(1, HSZ), (8, HSZ))

    for d in range(1, REACH):
        st_hop(d - 1).wait_recv()
        st_hop(d).start()
        rms_d[...] = column(stats_next[d - 1, 2 * heads : 2 * heads + 1, :], 2 * BLK)
        pull_d[...] = column(stats_next[d - 1, 2 * heads + 1 : 2 * heads + 2, :], 2 * BLK)

        def backward(h, d=d):
            delta = stats_own[pl.ds(heads + h, 1), :]
            dscore = (s_ref[d, h] * (nt(vb[d, h], db[h]) - delta)).astype(BF16)
            dq_acc[h] += tn(dscore, kb[d, h])
            grad_h = cotangent(
                ab[d, h], gb[d, h], gain_rows[h, 0:1, :], rms_d[...], pull_d[...]
            )
            log_total = stats_next[d - 1, pl.ds(h, 1), :]
            delta = stats_next[d - 1, pl.ds(heads + h, 1), :]
            weights = jnp.exp(r_ref[d - 1, h] - log_total)
            dv_acc[h] += nn(weights.astype(BF16), grad_h)
            dscore = (weights * (nt(vb[0, h], grad_h) - delta)).astype(BF16)
            dk_acc[h] += nn(dscore, qb[d, h])

        over_heads(backward)
        if d - 1 < len(stages):
            gain_end(d - 1)
            if d < len(stages):
                gain_begin(d)

    st_hop(3).wait_recv()
    for h in range(heads):
        cols = slice(h * HSZ, (h + 1) * HSZ)
        delta = stats_own[heads + h : heads + h + 1, 0:BLK]
        dscore = (s4_ref[h] * (nt(v4[h], db[h, 0:BLK, :]) - delta)).astype(BF16)
        dq_acc[h, 0:BLK, :] += tn(dscore, k4[h])
        dq_ref[:, cols] = (dq_acc[h] * factor).astype(BF16)
    rms = column(stats_next[3, 2 * heads : 2 * heads + 1, 0:BLK], BLK)
    pull = column(stats_next[3, 2 * heads + 1 : 2 * heads + 2, 0:BLK], BLK)
    for h in range(heads):
        cols = slice(h * HSZ, (h + 1) * HSZ)
        g_hop(3, h).wait_recv()
        a_hop(3, h).wait_recv()
        log_total = stats_next[3, h : h + 1, 0:BLK]
        delta = stats_next[3, heads + h : heads + h + 1, 0:BLK]
        weights = jnp.exp(r4_ref[h] - log_total)
        grad_h = cotangent(a4[h], g4[h], gain_rows[h, 0:1, :], rms, pull)
        dv_acc[h, BLK : 2 * BLK, :] += nn(weights.astype(BF16), grad_h)
        dscore = (weights * (nt(vb[0, h, BLK : 2 * BLK, :], grad_h) - delta)).astype(BF16)
        dk_acc[h, BLK : 2 * BLK, :] += nn(dscore, q4[h])
        dk_ref[:, cols] = (dk_acc[h] * factor).astype(BF16)
        dv_ref[:, cols] = dv_acc[h].astype(BF16)
        dgain_ref[0:1, cols] = gain_own[len(stages), h : h + 1, :]

    for hop in range(REACH):
        ip_hop(hop).wait_send()
        in_hop(hop).wait_send()
        st_hop(hop).wait_send()
        for h in range(heads):
            k_hop(hop, h).wait_send()
            q_hop(hop, h).wait_send()
            v_hop(hop, h).wait_send()
            g_hop(hop, h).wait_send()
            a_hop(hop, h).wait_send()
    for off in range(1, n_head):
        head_copy(off).wait_send()
    for stage, (_, radix) in enumerate(stages):
        for off in range(1, radix):
            gain_copy(stage, off).wait_send()


def put_out(*refs):
    ins, outs, sem = refs[:5], refs[5:10], refs[10]
    copies = [pltpu.make_async_copy(ins[i], outs[i], sem.at[i]) for i in range(4)]
    for one in copies:
        one.start()
    for h in range(outs[4].shape[0] // HSZ):
        cols = slice(h * HSZ, (h + 1) * HSZ)
        outs[4][cols] = ins[4][0:1, cols].reshape(HSZ)
    for one in copies:
        one.wait()


def body(queries, key_rows, value_rows, grad_normed, norm_gain, utter_ids):
    rows, width = queries.shape
    heads = width // HSZ
    n_tm, n_head = lax.axis_size("tm"), lax.axis_size("head")
    stages = radices(n_tm)
    full = pltpu.VMEM((REACH, heads, rows, HSZ), BF16)
    last = pltpu.VMEM((heads, BLK, HSZ), BF16)
    wide = pltpu.VMEM((heads, rows, HSZ), F32)
    dma = pltpu.SemaphoreType.DMA
    hops = [dma((REACH, heads))] * 10 + [dma((REACH,))] * 6
    most = max(radix for _, radix in stages) - 1
    scratch = [full] * 5 + [last] * 5
    scratch += [
        pltpu.VMEM((heads, rows, HSZ), BF16),
        pltpu.VMEM((8, BLK), jnp.int32),
        pltpu.VMEM((REACH, 8, BLK), jnp.int32),
        pltpu.VMEM((REACH, 8, BLK), jnp.int32),
        pltpu.VMEM((8, rows), F32),
        pltpu.VMEM((REACH, 8, rows), F32),
        pltpu.VMEM((REACH, heads, rows, rows), F32),
        pltpu.VMEM((heads, BLK, BLK), F32),
        pltpu.VMEM((REACH - 1, heads, rows, rows), F32),
        pltpu.VMEM((heads, BLK, BLK), F32),
        wide,
        pltpu.VMEM((8, rows), F32),
        pltpu.VMEM((n_head - 1, 8, rows), F32),
        pltpu.VMEM((len(stages) + 1, 8, HSZ), F32),
        pltpu.VMEM((len(stages), most, 8, HSZ), F32),
        wide,
        wide,
        wide,
        pltpu.VMEM((heads, 8, HSZ), F32),
        pltpu.VMEM((rows, HSZ), F32),
        pltpu.VMEM((rows, HSZ), F32),
        dma((4, heads)),
    ]
    scratch += hops
    scratch += [dma((n_head - 1,))] * 2 + [dma((len(stages), most))] * 2
    hbm = pl.BlockSpec(memory_space=pl.ANY)
    vmem = pl.BlockSpec(memory_space=pltpu.VMEM)
    big = jax.ShapeDtypeStruct((rows, width), BF16)
    outs = pl.pallas_call(
        functools.partial(kernel, n_tm, n_head, heads, stages),
        out_shape=[big] * 4 + [jax.ShapeDtypeStruct((1, width), F32)],
        in_specs=[hbm] * 4 + [vmem, pl.BlockSpec(memory_space=pltpu.SMEM)],
        out_specs=[vmem] * 5,
        scratch_shapes=scratch,
        compiler_params=pltpu.CompilerParams(collective_id=0, has_side_effects=True),
        name="attention_step",
    )(queries, key_rows, value_rows, grad_normed, norm_gain, utter_ids)
    return tuple(
        pl.pallas_call(
            put_out,
            out_shape=[big] * 4 + [jax.ShapeDtypeStruct((width,), F32)],
            in_specs=[vmem] * 5,
            out_specs=[hbm] * 4 + [vmem],
            scratch_shapes=[dma((4,))],
            name="put_out",
        )(*outs)
    )


def solution(mesh):
    in_specs = (
        P("tm", "head"),
        P("tm", "head"),
        P("tm", "head"),
        P("tm", "head"),
        P("head"),
        P("tm"),
    )
    out_specs = (P("tm", "head"), P("tm", "head"), P("tm", "head"), P("tm", "head"), P("head"))
    return jax.shard_map(body, mesh=mesh, in_specs=in_specs, out_specs=out_specs, check_vma=False)
```

```python
import functools

import jax
import jax.numpy as jnp
from jax import lax
from jax.experimental import pallas as pl
from jax.experimental.pallas import tpu as pltpu
from jax.sharding import PartitionSpec as P

HSZ = 128
BLK = 128
REACH = 4
NEG = -1e30
MESH = pl.DeviceIdType.MESH
F32 = jnp.float32
BF16 = jnp.bfloat16


def nt(a, b):
    return lax.dot_general(a, b, (((1,), (1,)), ((), ())), preferred_element_type=F32)


def tn(a, b):
    return lax.dot_general(a, b, (((0,), (0,)), ((), ())), preferred_element_type=F32)


def nn(a, b):
    return lax.dot_general(a, b, (((1,), (0,)), ((), ())), preferred_element_type=F32)


def radices(count):
    found, stride = [], 1
    while stride < count:
        radix = min(4, count // stride)
        found.append((stride, radix))
        stride *= radix
    return found


def kernel(
    n_tm,
    n_head,
    heads,
    stages,
    q_hbm,
    k_hbm,
    v_hbm,
    g_hbm,
    gain_ref,
    ids_ref,
    normed_ref,
    dq_ref,
    dk_ref,
    dv_ref,
    dgain_ref,
    qb,
    kb,
    vb,
    gb,
    ab,
    q4,
    k4,
    v4,
    g4,
    a4,
    db,
    ids_own,
    ids_prev,
    ids_next,
    stats_own,
    stats_next,
    ls_own,
    ls_next,
    s_ref,
    s4_ref,
    r_ref,
    r4_ref,
    out_acc,
    sums_own,
    sums_in,
    gain_own,
    gain_in,
    dq_acc,
    dk_acc,
    dv_acc,
    gain_rows,
    rms_d,
    pull_d,
    local_sem,
    k_send,
    k_recv,
    q_send,
    q_recv,
    v_send,
    v_recv,
    g_send,
    g_recv,
    a_send,
    a_recv,
    ip_send,
    ip_recv,
    in_send,
    in_recv,
    st_send,
    st_recv,
    ls_send,
    ls_recv,
    hd_send,
    hd_recv,
    gn_send,
    gn_recv,
):
    tm = lax.axis_index("tm")
    head = lax.axis_index("head")
    later = (lax.rem(tm + 1, n_tm), head)
    earlier = (lax.rem(tm + n_tm - 1, n_tm), head)
    factor = HSZ ** (-0.5)
    features = HSZ * heads * n_head

    def local(which, src, dst, h):
        return pltpu.make_async_copy(
            src.at[:, h * HSZ : (h + 1) * HSZ], dst.at[h], local_sem.at[which, h]
        )

    loads = []
    for which, (src, dst) in enumerate(
        [(k_hbm, kb.at[0]), (q_hbm, qb.at[0]), (v_hbm, vb.at[0]), (g_hbm, gb.at[0])]
    ):
        loads.append([local(which, src, dst, h) for h in range(heads)])
        for one in loads[-1]:
            one.start()

    ids_own[...] = jnp.zeros(ids_own.shape, jnp.int32)
    ids_own[0:1, :] = jnp.full((1, BLK), ids_ref[0], jnp.int32)
    ids_own[1:2, :] = jnp.full((1, BLK), ids_ref[1], jnp.int32)

    def gain_peer(stage, off):
        stride, radix = stages[stage]
        digit = lax.rem(tm // stride, radix)
        return (tm + (lax.rem(digit + off, radix) - digit) * stride, head)

    barrier = pltpu.get_barrier_semaphore()
    greeted = [later, earlier]
    greeted += [(tm, lax.rem(head + off, n_head)) for off in range(1, n_head)]
    for stage, (_, radix) in enumerate(stages):
        greeted += [gain_peer(stage, off) for off in range(1, radix)]
    for peer in greeted:
        pl.semaphore_signal(barrier, inc=1, device_id=peer, device_id_type=MESH)
    pl.semaphore_wait(barrier, len(greeted))

    def remote(src, dst, send, recv, peer):
        return pltpu.make_async_remote_copy(
            src_ref=src,
            dst_ref=dst,
            send_sem=send,
            recv_sem=recv,
            device_id=peer,
            device_id_type=MESH,
        )

    def chain(full, last, send, recv, peer, rows, hop, h):
        if hop < REACH - 1:
            src, dst = full.at[hop, h], full.at[hop + 1, h]
        else:
            src, dst = full.at[hop, h, rows, :], last.at[h]
        return remote(src, dst, send.at[hop, h], recv.at[hop, h], peer)

    low, high = pl.ds(0, BLK), pl.ds(BLK, BLK)
    k_hop = functools.partial(chain, kb, k4, k_send, k_recv, later, high)
    v_hop = functools.partial(chain, vb, v4, v_send, v_recv, later, high)
    q_hop = functools.partial(chain, qb, q4, q_send, q_recv, earlier, low)
    g_hop = functools.partial(chain, gb, g4, g_send, g_recv, earlier, low)
    a_hop = functools.partial(chain, ab, a4, a_send, a_recv, earlier, low)

    def small_hop(own, got, send, recv, peer, hop):
        src = own if hop == 0 else got.at[hop - 1]
        return remote(src, got.at[hop], send.at[hop], recv.at[hop], peer)

    ip_hop = functools.partial(small_hop, ids_own, ids_prev, ip_send, ip_recv, later)
    in_hop = functools.partial(small_hop, ids_own, ids_next, in_send, in_recv, earlier)
    ls_hop = functools.partial(small_hop, ls_own, ls_next, ls_send, ls_recv, earlier)
    st_hop = functools.partial(small_hop, stats_own, stats_next, st_send, st_recv, earlier)

    def over_heads(step):
        lax.fori_loop(0, heads, lambda h, c: (step(h), c)[1], 0)

    def bias_row(key_row, query_rows):
        parts = [jnp.where(key_row == row, 0.0, NEG).astype(F32) for row in query_rows]
        return parts[0] if len(parts) == 1 else jnp.concatenate(parts, axis=1)

    ip_hop(0).start()
    in_hop(0).start()
    for h in range(heads):
        loads[0][h].wait()
        k_hop(0, h).start()
        loads[1][h].wait()
        q_hop(0, h).start()

    own_rows = [ids_own[0:1, :], ids_own[1:2, :]]

    def score_block(dst, keys, queries, biases):
        for part in range(2):
            rows = pl.ds(part * BLK, BLK)
            dst[rows, :] = nt(keys[rows, :], queries[...]) * factor + biases[part]

    own_bias = [bias_row(own_rows[p], own_rows) for p in range(2)]
    over_heads(lambda h: score_block(s_ref.at[0, h], kb.at[0, h], qb.at[0, h], own_bias))

    for d in range(1, REACH):
        ip_hop(d - 1).wait_recv()
        ip_hop(d).start()
        in_hop(d - 1).wait_recv()
        in_hop(d).start()
        prev_rows = [ids_prev[d - 1, 0:1, :], ids_prev[d - 1, 1:2, :]]
        next_rows = [ids_next[d - 1, 0:1, :], ids_next[d - 1, 1:2, :]]
        s_bias = [bias_row(prev_rows[p], own_rows) for p in range(2)]
        r_bias = [bias_row(own_rows[p], next_rows) for p in range(2)]

        def arrive(h, d=d, s_bias=s_bias, r_bias=r_bias):
            k_hop(d - 1, h).wait_recv()
            k_hop(d, h).start()
            q_hop(d - 1, h).wait_recv()
            q_hop(d, h).start()
            score_block(s_ref.at[d, h], kb.at[d, h], qb.at[0, h], s_bias)
            score_block(r_ref.at[d - 1, h], kb.at[0, h], qb.at[d, h], r_bias)

        over_heads(arrive)

    for h in range(heads):
        loads[2][h].wait()
        v_hop(0, h).start()
        loads[3][h].wait()
        g_hop(0, h).start()
    ip_hop(3).wait_recv()
    in_hop(3).wait_recv()
    s4_bias = bias_row(ids_prev[3, 1:2, :], [own_rows[0]])
    r4_bias = bias_row(own_rows[1], [ids_next[3, 0:1, :]])

    def soften(h):
        k_hop(3, h).wait_recv()
        q_hop(3, h).wait_recv()
        s4 = nt(k4[h], qb[0, h, 0:BLK, :]) * factor + s4_bias
        r4_ref[h] = nt(kb[0, h, BLK : 2 * BLK, :], q4[h]) * factor + r4_bias
        top = jnp.max(s_ref[0, h], axis=0, keepdims=True)
        for d in range(1, REACH):
            top = jnp.maximum(top, jnp.max(s_ref[d, h], axis=0, keepdims=True))
        top4 = jnp.max(s4, axis=0, keepdims=True)
        top_low = jnp.maximum(top[:, 0:BLK], top4)
        top = jnp.concatenate([top_low, top[:, BLK:]], axis=1)
        e4 = jnp.exp(s4 - top_low)
        total4 = jnp.sum(e4, axis=0, keepdims=True)
        total = jnp.concatenate([total4, jnp.zeros((1, BLK), F32)], axis=1)
        for d in range(REACH):
            e = jnp.exp(s_ref[d, h] - top)
            s_ref[d, h] = e
            total = total + jnp.sum(e, axis=0, keepdims=True)
        inverse = 1.0 / total
        for d in range(REACH):
            s_ref[d, h] = s_ref[d, h] * inverse
        s4_ref[h] = e4 * inverse[:, 0:BLK]
        ls_own[pl.ds(h, 1), :] = top + jnp.log(total)
        out_acc[h] = tn(s_ref[0, h].astype(BF16), vb[0, h])

    stats_own[...] = jnp.zeros(stats_own.shape, F32)
    ls_own[...] = jnp.zeros(ls_own.shape, F32)
    over_heads(soften)
    ls_hop(0).start()

    for d in range(1, REACH):
        ls_hop(d - 1).wait_recv()
        ls_hop(d).start()

        def attend(h, d=d):
            v_hop(d - 1, h).wait_recv()
            v_hop(d, h).start()
            g_hop(d - 1, h).wait_recv()
            g_hop(d, h).start()
            out_acc[h] += tn(s_ref[d, h].astype(BF16), vb[d, h])
            r_ref[d - 1, h] = jnp.exp(r_ref[d - 1, h] - ls_next[d - 1, pl.ds(h, 1), :])

        over_heads(attend)

    square = jnp.zeros((2 * BLK, HSZ), F32)
    cross = jnp.zeros((2 * BLK, HSZ), F32)
    for h in range(heads):
        v_hop(3, h).wait_recv()
        out_acc[h, 0:BLK, :] += tn(s4_ref[h].astype(BF16), v4[h])
        att_b = out_acc[h].astype(BF16)
        ab[0, h] = att_b
        att = att_b.astype(F32)
        scaled = gb[0, h].astype(F32) * gain_ref[h * HSZ : (h + 1) * HSZ].reshape(1, HSZ)
        square = square + att * att
        cross = cross + scaled * att
        a_hop(0, h).start()
    sums_own[...] = jnp.zeros(sums_own.shape, F32)
    sums_own[0:1, :] = jnp.sum(square.T, axis=0, keepdims=True)
    sums_own[1:2, :] = jnp.sum(cross.T, axis=0, keepdims=True)

    def head_copy(off):
        return remote(
            sums_own,
            sums_in.at[off - 1],
            hd_send.at[off - 1],
            hd_recv.at[off - 1],
            (tm, lax.rem(head + off, n_head)),
        )

    for off in range(1, n_head):
        head_copy(off).start()
    ls_hop(3).wait_recv()
    for h in range(heads):
        r4_ref[h] = jnp.exp(r4_ref[h] - ls_next[3, h : h + 1, 0:BLK])
        a_hop(0, h).wait_recv()
        a_hop(1, h).start()
    sums = sums_own[...]
    for off in range(1, n_head):
        head_copy(off).wait_recv()
        sums = sums + sums_in[off - 1]
    rms_row = 1.0 / jnp.sqrt(sums[0:1, :] / features + 1e-06)
    pull_row = rms_row * rms_row * sums[1:2, :] / features
    stats_own[2 * heads : 2 * heads + 1, :] = rms_row
    stats_own[2 * heads + 1 : 2 * heads + 2, :] = pull_row

    def column(row, count):
        return jnp.broadcast_to(row, (HSZ, count)).T

    def cotangent(att_b, grad_b, gain, rms, pull):
        return (rms * (grad_b.astype(F32) * gain - att_b.astype(F32) * pull)).astype(BF16)

    rms = column(rms_row, 2 * BLK)
    pull = column(pull_row, 2 * BLK)
    for h in range(heads):
        gain = gain_ref[h * HSZ : (h + 1) * HSZ].reshape(1, HSZ)
        att_b = ab[0, h]
        grad_att = cotangent(att_b, gb[0, h], gain, rms, pull)
        db[h] = grad_att
        delta = att_b.astype(F32) * grad_att.astype(F32)
        stats_own[heads + h : heads + h + 1, :] = jnp.sum(delta.T, axis=0, keepdims=True)
    st_hop(0).start()
    gain_own[...] = jnp.zeros(gain_own.shape, F32)
    for h in range(heads):
        a_hop(1, h).wait_recv()
        a_hop(2, h).start()
        cols = slice(h * HSZ, (h + 1) * HSZ)
        scaled_att = ab[0, h].astype(F32) * rms
        normed_ref[:, cols] = (scaled_att * gain_ref[cols].reshape(1, HSZ)).astype(BF16)
        gain_own[0, h : h + 1, :] = jnp.sum(
            gb[0, h].astype(F32) * scaled_att, axis=0, keepdims=True
        )

    def gain_copy(stage, off):
        return remote(
            gain_own.at[stage],
            gain_in.at[stage, off - 1],
            gn_send.at[stage, off - 1],
            gn_recv.at[stage, off - 1],
            gain_peer(stage, off),
        )

    def gain_begin(stage):
        for off in range(1, stages[stage][1]):
            gain_copy(stage, off).start()

    def gain_end(stage):
        total = gain_own[stage]
        for off in range(1, stages[stage][1]):
            gain_copy(stage, off).wait_recv()
            total = total + gain_in[stage, off - 1]
        gain_own[stage + 1] = total

    gain_begin(0)

    def own_block(h):
        weights = s_ref[0, h]
        grad_h = db[h]
        delta = stats_own[pl.ds(heads + h, 1), :]
        dscore = (weights * (nt(vb[0, h], grad_h) - delta)).astype(BF16)
        dq_acc[h] = tn(dscore, kb[0, h])
        dk_acc[h] = nn(dscore, qb[0, h])
        dv_acc[h] = nn(weights.astype(BF16), grad_h)

    over_heads(own_block)

    for h in range(heads):
        cols = slice(h * HSZ, (h + 1) * HSZ)
        gain_rows[h] = jnp.broadcast_to(gain_ref[cols].reshape(1, HSZ), (8, HSZ))

    for d in range(1, REACH):
        st_hop(d - 1).wait_recv()
        st_hop(d).start()
        rms_d[...] = column(stats_next[d - 1, 2 * heads : 2 * heads + 1, :], 2 * BLK)
        pull_d[...] = column(stats_next[d - 1, 2 * heads + 1 : 2 * heads + 2, :], 2 * BLK)

        def backward(h, d=d):
            if d == 1:
                a_hop(2, h).wait_recv()
                a_hop(3, h).start()
            delta = stats_own[pl.ds(heads + h, 1), :]
            dscore = (s_ref[d, h] * (nt(vb[d, h], db[h]) - delta)).astype(BF16)
            dq_acc[h] += tn(dscore, kb[d, h])
            grad_h = cotangent(
                ab[d, h], gb[d, h], gain_rows[h, 0:1, :], rms_d[...], pull_d[...]
            )
            delta = stats_next[d - 1, pl.ds(heads + h, 1), :]
            weights = r_ref[d - 1, h]
            dv_acc[h] += nn(weights.astype(BF16), grad_h)
            dscore = (weights * (nt(vb[0, h], grad_h) - delta)).astype(BF16)
            dk_acc[h] += nn(dscore, qb[d, h])

        over_heads(backward)
        if d - 1 < len(stages):
            gain_end(d - 1)
            if d < len(stages):
                gain_begin(d)

    st_hop(3).wait_recv()
    for h in range(heads):
        cols = slice(h * HSZ, (h + 1) * HSZ)
        delta = stats_own[heads + h : heads + h + 1, 0:BLK]
        dscore = (s4_ref[h] * (nt(v4[h], db[h, 0:BLK, :]) - delta)).astype(BF16)
        dq_acc[h, 0:BLK, :] += tn(dscore, k4[h])
        dq_ref[:, cols] = (dq_acc[h] * factor).astype(BF16)
    rms = column(stats_next[3, 2 * heads : 2 * heads + 1, 0:BLK], BLK)
    pull = column(stats_next[3, 2 * heads + 1 : 2 * heads + 2, 0:BLK], BLK)
    for h in range(heads):
        cols = slice(h * HSZ, (h + 1) * HSZ)
        g_hop(3, h).wait_recv()
        a_hop(3, h).wait_recv()
        delta = stats_next[3, heads + h : heads + h + 1, 0:BLK]
        weights = r4_ref[h]
        grad_h = cotangent(a4[h], g4[h], gain_rows[h, 0:1, :], rms, pull)
        dv_acc[h, BLK : 2 * BLK, :] += nn(weights.astype(BF16), grad_h)
        dscore = (weights * (nt(vb[0, h, BLK : 2 * BLK, :], grad_h) - delta)).astype(BF16)
        dk_acc[h, BLK : 2 * BLK, :] += nn(dscore, q4[h])
        dk_ref[:, cols] = (dk_acc[h] * factor).astype(BF16)
        dv_ref[:, cols] = dv_acc[h].astype(BF16)
        dgain_ref[0:1, cols] = gain_own[len(stages), h : h + 1, :]

    for hop in range(REACH):
        ip_hop(hop).wait_send()
        in_hop(hop).wait_send()
        st_hop(hop).wait_send()
        ls_hop(hop).wait_send()
        for h in range(heads):
            k_hop(hop, h).wait_send()
            q_hop(hop, h).wait_send()
            v_hop(hop, h).wait_send()
            g_hop(hop, h).wait_send()
            a_hop(hop, h).wait_send()
    for off in range(1, n_head):
        head_copy(off).wait_send()
    for stage, (_, radix) in enumerate(stages):
        for off in range(1, radix):
            gain_copy(stage, off).wait_send()


def put_out(*refs):
    ins, outs, sem = refs[:5], refs[5:10], refs[10]
    copies = [pltpu.make_async_copy(ins[i], outs[i], sem.at[i]) for i in range(4)]
    for one in copies:
        one.start()
    for h in range(outs[4].shape[0] // HSZ):
        cols = slice(h * HSZ, (h + 1) * HSZ)
        outs[4][cols] = ins[4][0:1, cols].reshape(HSZ)
    for one in copies:
        one.wait()


def body(queries, key_rows, value_rows, grad_normed, norm_gain, utter_ids):
    rows, width = queries.shape
    heads = width // HSZ
    n_tm, n_head = lax.axis_size("tm"), lax.axis_size("head")
    stages = radices(n_tm)
    full = pltpu.VMEM((REACH, heads, rows, HSZ), BF16)
    last = pltpu.VMEM((heads, BLK, HSZ), BF16)
    wide = pltpu.VMEM((heads, rows, HSZ), F32)
    dma = pltpu.SemaphoreType.DMA
    hops = [dma((REACH, heads))] * 10 + [dma((REACH,))] * 8
    most = max(radix for _, radix in stages) - 1
    scratch = [full] * 5 + [last] * 5
    scratch += [
        pltpu.VMEM((heads, rows, HSZ), BF16),
        pltpu.VMEM((8, BLK), jnp.int32),
        pltpu.VMEM((REACH, 8, BLK), jnp.int32),
        pltpu.VMEM((REACH, 8, BLK), jnp.int32),
        pltpu.VMEM((8, rows), F32),
        pltpu.VMEM((REACH, 8, rows), F32),
        pltpu.VMEM((8, rows), F32),
        pltpu.VMEM((REACH, 8, rows), F32),
        pltpu.VMEM((REACH, heads, rows, rows), F32),
        pltpu.VMEM((heads, BLK, BLK), F32),
        pltpu.VMEM((REACH - 1, heads, rows, rows), F32),
        pltpu.VMEM((heads, BLK, BLK), F32),
        wide,
        pltpu.VMEM((8, rows), F32),
        pltpu.VMEM((n_head - 1, 8, rows), F32),
        pltpu.VMEM((len(stages) + 1, 8, HSZ), F32),
        pltpu.VMEM((len(stages), most, 8, HSZ), F32),
        wide,
        wide,
        wide,
        pltpu.VMEM((heads, 8, HSZ), F32),
        pltpu.VMEM((rows, HSZ), F32),
        pltpu.VMEM((rows, HSZ), F32),
        dma((4, heads)),
    ]
    scratch += hops
    scratch += [dma((n_head - 1,))] * 2 + [dma((len(stages), most))] * 2
    hbm = pl.BlockSpec(memory_space=pl.ANY)
    vmem = pl.BlockSpec(memory_space=pltpu.VMEM)
    big = jax.ShapeDtypeStruct((rows, width), BF16)
    outs = pl.pallas_call(
        functools.partial(kernel, n_tm, n_head, heads, stages),
        out_shape=[big] * 4 + [jax.ShapeDtypeStruct((1, width), F32)],
        in_specs=[hbm] * 4 + [vmem, pl.BlockSpec(memory_space=pltpu.SMEM)],
        out_specs=[vmem] * 5,
        scratch_shapes=scratch,
        compiler_params=pltpu.CompilerParams(collective_id=0, has_side_effects=True),
        name="attention_step",
    )(queries, key_rows, value_rows, grad_normed, norm_gain, utter_ids)
    return tuple(
        pl.pallas_call(
            put_out,
            out_shape=[big] * 4 + [jax.ShapeDtypeStruct((width,), F32)],
            in_specs=[vmem] * 5,
            out_specs=[hbm] * 4 + [vmem],
            scratch_shapes=[dma((4,))],
            name="put_out",
        )(*outs)
    )


def solution(mesh):
    in_specs = (
        P("tm", "head"),
        P("tm", "head"),
        P("tm", "head"),
        P("tm", "head"),
        P("head"),
        P("tm"),
    )
    out_specs = (P("tm", "head"), P("tm", "head"), P("tm", "head"), P("tm", "head"), P("head"))
    return jax.shard_map(body, mesh=mesh, in_specs=in_specs, out_specs=out_specs, check_vma=False)
```

```python
import functools

import jax
import jax.numpy as jnp
from jax import lax
from jax.experimental import pallas as pl
from jax.experimental.pallas import tpu as pltpu
from jax.sharding import PartitionSpec as P

HSZ = 128
BLK = 128
REACH = 4
NEG = -1e30
MESH = pl.DeviceIdType.MESH
F32 = jnp.float32
BF16 = jnp.bfloat16


def nt(a, b):
    return lax.dot_general(a, b, (((1,), (1,)), ((), ())), preferred_element_type=F32)


def tn(a, b):
    return lax.dot_general(a, b, (((0,), (0,)), ((), ())), preferred_element_type=F32)


def nn(a, b):
    return lax.dot_general(a, b, (((1,), (0,)), ((), ())), preferred_element_type=F32)


def radices(count):
    found, stride = [], 1
    while stride < count:
        radix = min(4, count // stride)
        found.append((stride, radix))
        stride *= radix
    return found


def kernel(
    n_tm,
    n_head,
    heads,
    stages,
    q_hbm,
    k_hbm,
    v_hbm,
    g_hbm,
    gain_ref,
    ids_ref,
    normed_ref,
    dq_ref,
    dk_ref,
    dv_ref,
    dgain_ref,
    qb,
    kb,
    vb,
    gb,
    ab,
    q4,
    k4,
    v4,
    g4,
    a4,
    db,
    ids_own,
    ids_prev,
    ids_next,
    stats_own,
    stats_next,
    s_ref,
    s4_ref,
    r_ref,
    r4_ref,
    out_acc,
    sums_own,
    sums_in,
    gain_own,
    gain_in,
    dq_acc,
    dk_acc,
    dv_acc,
    gain_rows,
    rms_d,
    pull_d,
    local_sem,
    k_send,
    k_recv,
    q_send,
    q_recv,
    v_send,
    v_recv,
    g_send,
    g_recv,
    a_send,
    a_recv,
    ip_send,
    ip_recv,
    in_send,
    in_recv,
    st_send,
    st_recv,
    hd_send,
    hd_recv,
    gn_send,
    gn_recv,
):
    tm = lax.axis_index("tm")
    head = lax.axis_index("head")
    later = (lax.rem(tm + 1, n_tm), head)
    earlier = (lax.rem(tm + n_tm - 1, n_tm), head)
    factor = HSZ ** (-0.5)
    features = HSZ * heads * n_head

    def local(which, src, dst, h):
        return pltpu.make_async_copy(
            src.at[:, h * HSZ : (h + 1) * HSZ], dst.at[h], local_sem.at[which, h]
        )

    loads = []
    for which, (src, dst) in enumerate(
        [(k_hbm, kb.at[0]), (q_hbm, qb.at[0]), (v_hbm, vb.at[0]), (g_hbm, gb.at[0])]
    ):
        loads.append([local(which, src, dst, h) for h in range(heads)])
        for one in loads[-1]:
            one.start()

    ids_own[...] = jnp.zeros(ids_own.shape, jnp.int32)
    ids_own[0:1, :] = jnp.full((1, BLK), ids_ref[0], jnp.int32)
    ids_own[1:2, :] = jnp.full((1, BLK), ids_ref[1], jnp.int32)

    def gain_peer(stage, off):
        stride, radix = stages[stage]
        digit = lax.rem(tm // stride, radix)
        return (tm + (lax.rem(digit + off, radix) - digit) * stride, head)

    barrier = pltpu.get_barrier_semaphore()
    greeted = [later, earlier]
    greeted += [(tm, lax.rem(head + off, n_head)) for off in range(1, n_head)]
    for stage, (_, radix) in enumerate(stages):
        greeted += [gain_peer(stage, off) for off in range(1, radix)]
    for peer in greeted:
        pl.semaphore_signal(barrier, inc=1, device_id=peer, device_id_type=MESH)
    pl.semaphore_wait(barrier, len(greeted))

    def remote(src, dst, send, recv, peer):
        return pltpu.make_async_remote_copy(
            src_ref=src,
            dst_ref=dst,
            send_sem=send,
            recv_sem=recv,
            device_id=peer,
            device_id_type=MESH,
        )

    def chain(full, last, send, recv, peer, rows, hop, h):
        if hop < REACH - 1:
            src, dst = full.at[hop, h], full.at[hop + 1, h]
        else:
            src, dst = full.at[hop, h, rows, :], last.at[h]
        return remote(src, dst, send.at[hop, h], recv.at[hop, h], peer)

    low, high = pl.ds(0, BLK), pl.ds(BLK, BLK)
    k_hop = functools.partial(chain, kb, k4, k_send, k_recv, later, high)
    v_hop = functools.partial(chain, vb, v4, v_send, v_recv, later, high)
    q_hop = functools.partial(chain, qb, q4, q_send, q_recv, earlier, low)
    g_hop = functools.partial(chain, gb, g4, g_send, g_recv, earlier, low)
    a_hop = functools.partial(chain, ab, a4, a_send, a_recv, earlier, low)

    def small_hop(own, got, send, recv, peer, hop):
        src = own if hop == 0 else got.at[hop - 1]
        return remote(src, got.at[hop], send.at[hop], recv.at[hop], peer)

    ip_hop = functools.partial(small_hop, ids_own, ids_prev, ip_send, ip_recv, later)
    in_hop = functools.partial(small_hop, ids_own, ids_next, in_send, in_recv, earlier)
    st_hop = functools.partial(small_hop, stats_own, stats_next, st_send, st_recv, earlier)

    def over_heads(step):
        lax.fori_loop(0, heads, lambda h, c: (step(h), c)[1], 0)

    def bias_row(key_row, query_rows):
        parts = [jnp.where(key_row == row, 0.0, NEG).astype(F32) for row in query_rows]
        return parts[0] if len(parts) == 1 else jnp.concatenate(parts, axis=1)

    ip_hop(0).start()
    in_hop(0).start()
    for h in range(heads):
        loads[0][h].wait()
        k_hop(0, h).start()
        loads[1][h].wait()
        q_hop(0, h).start()

    own_rows = [ids_own[0:1, :], ids_own[1:2, :]]

    def score_block(dst, keys, queries, biases):
        for part in range(2):
            rows = pl.ds(part * BLK, BLK)
            dst[rows, :] = nt(keys[rows, :], queries[...]) * factor + biases[part]

    own_bias = [bias_row(own_rows[p], own_rows) for p in range(2)]
    over_heads(lambda h: score_block(s_ref.at[0, h], kb.at[0, h], qb.at[0, h], own_bias))

    for d in range(1, REACH):
        ip_hop(d - 1).wait_recv()
        ip_hop(d).start()
        in_hop(d - 1).wait_recv()
        in_hop(d).start()
        prev_rows = [ids_prev[d - 1, 0:1, :], ids_prev[d - 1, 1:2, :]]
        next_rows = [ids_next[d - 1, 0:1, :], ids_next[d - 1, 1:2, :]]
        s_bias = [bias_row(prev_rows[p], own_rows) for p in range(2)]
        r_bias = [bias_row(own_rows[p], next_rows) for p in range(2)]

        def arrive(h, d=d, s_bias=s_bias, r_bias=r_bias):
            k_hop(d - 1, h).wait_recv()
            k_hop(d, h).start()
            q_hop(d - 1, h).wait_recv()
            q_hop(d, h).start()
            score_block(s_ref.at[d, h], kb.at[d, h], qb.at[0, h], s_bias)
            score_block(r_ref.at[d - 1, h], kb.at[0, h], qb.at[d, h], r_bias)

        over_heads(arrive)

    for h in range(heads):
        loads[2][h].wait()
        v_hop(0, h).start()
        loads[3][h].wait()
        g_hop(0, h).start()
    ip_hop(3).wait_recv()
    in_hop(3).wait_recv()
    s4_bias = bias_row(ids_prev[3, 1:2, :], [own_rows[0]])
    r4_bias = bias_row(own_rows[1], [ids_next[3, 0:1, :]])

    def soften(h):
        k_hop(3, h).wait_recv()
        q_hop(3, h).wait_recv()
        s4 = nt(k4[h], qb[0, h, 0:BLK, :]) * factor + s4_bias
        r4_ref[h] = nt(kb[0, h, BLK : 2 * BLK, :], q4[h]) * factor + r4_bias
        top = jnp.max(s_ref[0, h], axis=0, keepdims=True)
        for d in range(1, REACH):
            top = jnp.maximum(top, jnp.max(s_ref[d, h], axis=0, keepdims=True))
        top4 = jnp.max(s4, axis=0, keepdims=True)
        top_low = jnp.maximum(top[:, 0:BLK], top4)
        top = jnp.concatenate([top_low, top[:, BLK:]], axis=1)
        e4 = jnp.exp(s4 - top_low)
        total4 = jnp.sum(e4, axis=0, keepdims=True)
        total = jnp.concatenate([total4, jnp.zeros((1, BLK), F32)], axis=1)
        for d in range(REACH):
            e = jnp.exp(s_ref[d, h] - top)
            s_ref[d, h] = e
            total = total + jnp.sum(e, axis=0, keepdims=True)
        inverse = 1.0 / total
        for d in range(REACH):
            s_ref[d, h] = s_ref[d, h] * inverse
        s4_ref[h] = e4 * inverse[:, 0:BLK]
        stats_own[pl.ds(h, 1), :] = top + jnp.log(total)
        out_acc[h] = tn(s_ref[0, h].astype(BF16), vb[0, h])

    stats_own[...] = jnp.zeros(stats_own.shape, F32)
    over_heads(soften)

    for d in range(1, REACH):

        def attend(h, d=d):
            v_hop(d - 1, h).wait_recv()
            v_hop(d, h).start()
            g_hop(d - 1, h).wait_recv()
            g_hop(d, h).start()
            out_acc[h] += tn(s_ref[d, h].astype(BF16), vb[d, h])

        over_heads(attend)

    square = jnp.zeros((2 * BLK, HSZ), F32)
    cross = jnp.zeros((2 * BLK, HSZ), F32)
    for h in range(heads):
        v_hop(3, h).wait_recv()
        out_acc[h, 0:BLK, :] += tn(s4_ref[h].astype(BF16), v4[h])
        att_b = out_acc[h].astype(BF16)
        ab[0, h] = att_b
        att = att_b.astype(F32)
        scaled = gb[0, h].astype(F32) * gain_ref[h * HSZ : (h + 1) * HSZ].reshape(1, HSZ)
        square = square + att * att
        cross = cross + scaled * att
        a_hop(0, h).start()
    sums_own[...] = jnp.zeros(sums_own.shape, F32)
    sums_own[0:1, :] = jnp.sum(square.T, axis=0, keepdims=True)
    sums_own[1:2, :] = jnp.sum(cross.T, axis=0, keepdims=True)

    def head_copy(off):
        return remote(
            sums_own,
            sums_in.at[off - 1],
            hd_send.at[off - 1],
            hd_recv.at[off - 1],
            (tm, lax.rem(head + off, n_head)),
        )

    for off in range(1, n_head):
        head_copy(off).start()
    for h in range(heads):
        a_hop(0, h).wait_recv()
        a_hop(1, h).start()
    sums = sums_own[...]
    for off in range(1, n_head):
        head_copy(off).wait_recv()
        sums = sums + sums_in[off - 1]
    rms_row = 1.0 / jnp.sqrt(sums[0:1, :] / features + 1e-06)
    pull_row = rms_row * rms_row * sums[1:2, :] / features
    stats_own[2 * heads : 2 * heads + 1, :] = rms_row
    stats_own[2 * heads + 1 : 2 * heads + 2, :] = pull_row

    def column(row, count):
        return jnp.broadcast_to(row, (HSZ, count)).T

    def cotangent(att_b, grad_b, gain, rms, pull):
        return (rms * (grad_b.astype(F32) * gain - att_b.astype(F32) * pull)).astype(BF16)

    rms = column(rms_row, 2 * BLK)
    pull = column(pull_row, 2 * BLK)
    for h in range(heads):
        gain = gain_ref[h * HSZ : (h + 1) * HSZ].reshape(1, HSZ)
        att_b = ab[0, h]
        grad_att = cotangent(att_b, gb[0, h], gain, rms, pull)
        db[h] = grad_att
        delta = att_b.astype(F32) * grad_att.astype(F32)
        stats_own[heads + h : heads + h + 1, :] = jnp.sum(delta.T, axis=0, keepdims=True)
    st_hop(0).start()
    gain_own[...] = jnp.zeros(gain_own.shape, F32)
    for h in range(heads):
        cols = slice(h * HSZ, (h + 1) * HSZ)
        scaled_att = ab[0, h].astype(F32) * rms
        normed_ref[:, cols] = (scaled_att * gain_ref[cols].reshape(1, HSZ)).astype(BF16)
        gain_own[0, h : h + 1, :] = jnp.sum(
            gb[0, h].astype(F32) * scaled_att, axis=0, keepdims=True
        )

    def gain_copy(stage, off):
        return remote(
            gain_own.at[stage],
            gain_in.at[stage, off - 1],
            gn_send.at[stage, off - 1],
            gn_recv.at[stage, off - 1],
            gain_peer(stage, off),
        )

    def gain_begin(stage):
        for off in range(1, stages[stage][1]):
            gain_copy(stage, off).start()

    def gain_end(stage):
        total = gain_own[stage]
        for off in range(1, stages[stage][1]):
            gain_copy(stage, off).wait_recv()
            total = total + gain_in[stage, off - 1]
        gain_own[stage + 1] = total

    gain_begin(0)

    def own_block(h):
        a_hop(1, h).wait_recv()
        a_hop(2, h).start()
        weights = s_ref[0, h]
        grad_h = db[h]
        delta = stats_own[pl.ds(heads + h, 1), :]
        dscore = (weights * (nt(vb[0, h], grad_h) - delta)).astype(BF16)
        dq_acc[h] = tn(dscore, kb[0, h])
        dk_acc[h] = nn(dscore, qb[0, h])
        dv_acc[h] = nn(weights.astype(BF16), grad_h)

    over_heads(own_block)

    for h in range(heads):
        cols = slice(h * HSZ, (h + 1) * HSZ)
        gain_rows[h] = jnp.broadcast_to(gain_ref[cols].reshape(1, HSZ), (8, HSZ))

    for d in range(1, REACH):
        st_hop(d - 1).wait_recv()
        st_hop(d).start()
        rms_d[...] = column(stats_next[d - 1, 2 * heads : 2 * heads + 1, :], 2 * BLK)
        pull_d[...] = column(stats_next[d - 1, 2 * heads + 1 : 2 * heads + 2, :], 2 * BLK)

        def backward(h, d=d):
            if d == 1:
                a_hop(2, h).wait_recv()
                a_hop(3, h).start()
            delta = stats_own[pl.ds(heads + h, 1), :]
            dscore = (s_ref[d, h] * (nt(vb[d, h], db[h]) - delta)).astype(BF16)
            dq_acc[h] += tn(dscore, kb[d, h])
            grad_h = cotangent(
                ab[d, h], gb[d, h], gain_rows[h, 0:1, :], rms_d[...], pull_d[...]
            )
            log_total = stats_next[d - 1, pl.ds(h, 1), :]
            delta = stats_next[d - 1, pl.ds(heads + h, 1), :]
            weights = jnp.exp(r_ref[d - 1, h] - log_total)
            dv_acc[h] += nn(weights.astype(BF16), grad_h)
            dscore = (weights * (nt(vb[0, h], grad_h) - delta)).astype(BF16)
            dk_acc[h] += nn(dscore, qb[d, h])

        over_heads(backward)
        if d - 1 < len(stages):
            gain_end(d - 1)
            if d < len(stages):
                gain_begin(d)

    st_hop(3).wait_recv()
    for h in range(heads):
        cols = slice(h * HSZ, (h + 1) * HSZ)
        delta = stats_own[heads + h : heads + h + 1, 0:BLK]
        dscore = (s4_ref[h] * (nt(v4[h], db[h, 0:BLK, :]) - delta)).astype(BF16)
        dq_acc[h, 0:BLK, :] += tn(dscore, k4[h])
        dq_ref[:, cols] = (dq_acc[h] * factor).astype(BF16)
    rms = column(stats_next[3, 2 * heads : 2 * heads + 1, 0:BLK], BLK)
    pull = column(stats_next[3, 2 * heads + 1 : 2 * heads + 2, 0:BLK], BLK)
    for h in range(heads):
        cols = slice(h * HSZ, (h + 1) * HSZ)
        g_hop(3, h).wait_recv()
        a_hop(3, h).wait_recv()
        log_total = stats_next[3, h : h + 1, 0:BLK]
        delta = stats_next[3, heads + h : heads + h + 1, 0:BLK]
        weights = jnp.exp(r4_ref[h] - log_total)
        grad_h = cotangent(a4[h], g4[h], gain_rows[h, 0:1, :], rms, pull)
        dv_acc[h, BLK : 2 * BLK, :] += nn(weights.astype(BF16), grad_h)
        dscore = (weights * (nt(vb[0, h, BLK : 2 * BLK, :], grad_h) - delta)).astype(BF16)
        dk_acc[h, BLK : 2 * BLK, :] += nn(dscore, q4[h])
        dk_ref[:, cols] = (dk_acc[h] * factor).astype(BF16)
        dv_ref[:, cols] = dv_acc[h].astype(BF16)
        dgain_ref[0:1, cols] = gain_own[len(stages), h : h + 1, :]

    for hop in range(REACH):
        ip_hop(hop).wait_send()
        in_hop(hop).wait_send()
        st_hop(hop).wait_send()
        for h in range(heads):
            k_hop(hop, h).wait_send()
            q_hop(hop, h).wait_send()
            v_hop(hop, h).wait_send()
            g_hop(hop, h).wait_send()
            a_hop(hop, h).wait_send()
    for off in range(1, n_head):
        head_copy(off).wait_send()
    for stage, (_, radix) in enumerate(stages):
        for off in range(1, radix):
            gain_copy(stage, off).wait_send()


def put_out(*refs):
    ins, outs, sem = refs[:5], refs[5:10], refs[10]
    copies = [pltpu.make_async_copy(ins[i], outs[i], sem.at[i]) for i in range(4)]
    for one in copies:
        one.start()
    for h in range(outs[4].shape[0] // HSZ):
        cols = slice(h * HSZ, (h + 1) * HSZ)
        outs[4][cols] = ins[4][0:1, cols].reshape(HSZ)
    for one in copies:
        one.wait()


def body(queries, key_rows, value_rows, grad_normed, norm_gain, utter_ids):
    rows, width = queries.shape
    heads = width // HSZ
    n_tm, n_head = lax.axis_size("tm"), lax.axis_size("head")
    stages = radices(n_tm)
    full = pltpu.VMEM((REACH, heads, rows, HSZ), BF16)
    last = pltpu.VMEM((heads, BLK, HSZ), BF16)
    wide = pltpu.VMEM((heads, rows, HSZ), F32)
    dma = pltpu.SemaphoreType.DMA
    hops = [dma((REACH, heads))] * 10 + [dma((REACH,))] * 6
    most = max(radix for _, radix in stages) - 1
    scratch = [full] * 5 + [last] * 5
    scratch += [
        pltpu.VMEM((heads, rows, HSZ), BF16),
        pltpu.VMEM((8, BLK), jnp.int32),
        pltpu.VMEM((REACH, 8, BLK), jnp.int32),
        pltpu.VMEM((REACH, 8, BLK), jnp.int32),
        pltpu.VMEM((8, rows), F32),
        pltpu.VMEM((REACH, 8, rows), F32),
        pltpu.VMEM((REACH, heads, rows, rows), F32),
        pltpu.VMEM((heads, BLK, BLK), F32),
        pltpu.VMEM((REACH - 1, heads, rows, rows), F32),
        pltpu.VMEM((heads, BLK, BLK), F32),
        wide,
        pltpu.VMEM((8, rows), F32),
        pltpu.VMEM((n_head - 1, 8, rows), F32),
        pltpu.VMEM((len(stages) + 1, 8, HSZ), F32),
        pltpu.VMEM((len(stages), most, 8, HSZ), F32),
        wide,
        wide,
        wide,
        pltpu.VMEM((heads, 8, HSZ), F32),
        pltpu.VMEM((rows, HSZ), F32),
        pltpu.VMEM((rows, HSZ), F32),
        dma((4, heads)),
    ]
    scratch += hops
    scratch += [dma((n_head - 1,))] * 2 + [dma((len(stages), most))] * 2
    hbm = pl.BlockSpec(memory_space=pl.ANY)
    vmem = pl.BlockSpec(memory_space=pltpu.VMEM)
    big = jax.ShapeDtypeStruct((rows, width), BF16)
    outs = pl.pallas_call(
        functools.partial(kernel, n_tm, n_head, heads, stages),
        out_shape=[big] * 4 + [jax.ShapeDtypeStruct((1, width), F32)],
        in_specs=[hbm] * 4 + [vmem, pl.BlockSpec(memory_space=pltpu.SMEM)],
        out_specs=[vmem] * 5,
        scratch_shapes=scratch,
        compiler_params=pltpu.CompilerParams(collective_id=0, has_side_effects=True),
        name="attention_step",
    )(queries, key_rows, value_rows, grad_normed, norm_gain, utter_ids)
    return tuple(
        pl.pallas_call(
            put_out,
            out_shape=[big] * 4 + [jax.ShapeDtypeStruct((width,), F32)],
            in_specs=[vmem] * 5,
            out_specs=[hbm] * 4 + [vmem],
            scratch_shapes=[dma((4,))],
            name="put_out",
        )(*outs)
    )


def solution(mesh):
    in_specs = (
        P("tm", "head"),
        P("tm", "head"),
        P("tm", "head"),
        P("tm", "head"),
        P("head"),
        P("tm"),
    )
    out_specs = (P("tm", "head"), P("tm", "head"), P("tm", "head"), P("tm", "head"), P("head"))
    return jax.shard_map(body, mesh=mesh, in_specs=in_specs, out_specs=out_specs, check_vma=False)
```
